32 devices in a mesh: shard: 4 (over z), tensor: 4 (over x, core), section: 2 (over y).
Axes of the slice: x: 2, y: 2, z: 4, core: 2. Of those that a mesh axis runs over, the one named last changes fastest.
Arguments:
- hidden_acts: bfloat16 [2, 10240, 4096], P('section', 'shard', 'tensor'), may hold values from -8 to 8
- out_grads: bfloat16 [2, 10240, 1024], P('section', 'shard'), may hold values from -8 to 8
- errors: float32 [2, 4, 1024, 4096], P('section', 'shard', None, 'tensor'), may hold values from -3 to 3
- factors: float32 [2, 32, 4096], P('section', None, 'tensor'), may hold values from -6 to 6
- whiten: float32 [2, 2, 32, 32], P('section'), may hold values from -1.5 to 3
- momentum: float32 [2, 1024, 4096], P('section', 'shard', 'tensor'), may hold values from -3 to 3
- master: float32 [2, 1024, 4096], P('section', 'shard', 'tensor'), may hold values from -3 to 3
- table: bfloat16 [32768, 1024], P(('shard', 'section'), 'tensor'), may hold values from -5 to 5
- touched_ids: int32 [1024], P(('shard', 'section')), may hold values from 0 to 32767, as said below
- touched_grads: bfloat16 [1024, 1024], P(('shard', 'section'), 'tensor'), may hold values from -5 to 5
Outputs:
- new_errors: float32 [2, 4, 1024, 4096], P('section', 'shard', None, 'tensor')
- new_factors: float32 [2, 32, 4096], P('section', None, 'tensor')
- new_momentum: float32 [2, 1024, 4096], P('section', 'shard', 'tensor')
- new_master: float32 [2, 1024, 4096], P('section', 'shard', 'tensor')
- new_weights: bfloat16 [2, 1024, 4096], P('section', None, 'tensor')
- new_table: bfloat16 [32768, 1024], P(('shard', 'section'), 'tensor')
The draws below stay inside these ranges and needn't reach their ends.
Inputs may be any that keep to these rules, and one draw needn't show every extreme that they name: `touched_ids`: the 128 ids of one device of shard and section name at most 32 rows in each block of 4096 vocabulary rows; in every draw one block receives exactly 32 rows from every device.
All inputs are finite; a program needn't handle non-finite values.
Results may differ from the reference program's by a relative error of at most 0.0036.
Values may be sent and summed in bfloat16 or wider, within the bound.
A program may use at most 128 MiB of HBM per device.

```python
import jax
import jax.numpy as jnp
from jax import lax

D = 1024
FF = 4096
R = 32
ROUNDS = 2
VOC_DEV = 4096
TOK_DEV = 2560
ROWS_DEV = 128
LAYERS = 2
TOKENS = 10240
OWNERS = 8
VOCAB = 32768
ROWS_ALL = 1024
CAP = 32
N_SHARD = 4


def draw_hidden_acts(key, part):
    noise_key = jax.random.fold_in(key, 0)
    column = jnp.arange(FF, dtype=jnp.float32) / FF
    col_scale = 0.5 * jnp.power(10.0, column - 0.5)
    base = jnp.clip(jax.random.normal(noise_key, (LAYERS, TOKENS, FF), jnp.float32), -4.0, 4.0)
    return (base * col_scale).astype(jnp.bfloat16)


def draw_out_grads(key, part):
    noise_key = jax.random.fold_in(jax.random.fold_in(key, 7), 0)
    column = jnp.arange(D, dtype=jnp.float32) / D
    col_scale = 0.5 * jnp.power(10.0, column - 0.5) / jnp.sqrt(jnp.float32(TOK_DEV))
    base = jnp.clip(jax.random.normal(noise_key, (LAYERS, TOKENS, D), jnp.float32), -4.0, 4.0)
    return (base * col_scale).astype(jnp.bfloat16)


def draw_whiten(key, part):
    diag_key, off_key = jax.random.split(jax.random.fold_in(key, 11))
    identity = jnp.eye(R, dtype=jnp.float32)
    diagonal = jax.random.uniform(diag_key, (LAYERS, ROUNDS, 1, R), jnp.float32, 0.7, 1.3)
    off_part = 0.25 * jnp.clip(jax.random.normal(off_key, (LAYERS, ROUNDS, R, R), jnp.float32), -4.0, 4.0)
    return identity * diagonal + off_part * (1.0 - identity)


def draw_touched_ids(key, part):
    capacity = CAP
    common_key, block_key = jax.random.split(jax.random.fold_in(key, 13))
    full_owner = jax.random.randint(common_key, (), 0, OWNERS, dtype=jnp.int32)

    def one_block(block_seed):
        slot_key, order_key, offset_key = jax.random.split(block_seed, 3)
        slot_list = jax.random.permutation(slot_key, (OWNERS - 1) * capacity).astype(jnp.int32)
        others = slot_list[:ROWS_DEV - capacity] // capacity
        others = others + (others >= full_owner).astype(jnp.int32)
        owners_of = jnp.concatenate([jnp.full((capacity,), full_owner, jnp.int32), others.astype(jnp.int32)])
        owners_of = jax.random.permutation(order_key, owners_of).astype(jnp.int32)
        offsets = jax.random.randint(offset_key, (ROWS_DEV,), 0, VOC_DEV, dtype=jnp.int32)
        return (owners_of * VOC_DEV + offsets).astype(jnp.int32)
    block_keys = jax.random.split(block_key, OWNERS)
    return jax.vmap(one_block)(block_keys).reshape(ROWS_ALL).astype(jnp.int32)


def block_levels(stream_key, shape, shards, smallest, high):
    level, own = 1.0, jax.random.fold_in(stream_key, 6)
    for dim, parts in shards:
        heights = jnp.exp(jax.random.uniform(jax.random.fold_in(own, dim), (parts,), jnp.float32, smallest / len(shards), high / len(shards)))
        level = level * jnp.repeat(heights, shape[dim] // parts).reshape([-1 if axis == dim else 1 for axis in range(len(shape))])
    return level


def scatter_about(own_key, shape, scale, most, cuts=(), kind=jnp.bfloat16):
    values = scale * jax.random.normal(own_key, shape, jnp.float32)
    if cuts:
        values = values * block_levels(own_key, shape, cuts, -0.22, 0.18)
    return jnp.clip(values, -most, most).astype(kind)


def setup_inputs(seed: int = 0) -> dict:
    key_list = jax.random.split(jax.random.key(seed), 11)
    hidden_acts = draw_hidden_acts(jax.random.fold_in(key_list[10], 71), 0)
    out_grads = draw_out_grads(jax.random.fold_in(key_list[10], 71), 0)
    errors = scatter_about(key_list[2], (LAYERS, N_SHARD, D, FF), 0.5, 3.0, ((0, 2), (1, 4), (3, 4)), jnp.float32)
    factors = scatter_about(key_list[3], (LAYERS, R, FF), 1.0, 6.0, ((0, 2), (2, 4)), jnp.float32)
    whiten = draw_whiten(jax.random.fold_in(key_list[10], 71), 0)
    momentum = scatter_about(key_list[5], (LAYERS, D, FF), 0.5, 3.0, ((0, 2), (1, 4), (2, 4)), jnp.float32)
    master = scatter_about(key_list[6], (LAYERS, D, FF), 0.5, 3.0, ((0, 2), (1, 4), (2, 4)), jnp.float32)
    table = scatter_about(key_list[7], (VOCAB, D), 1.0, 5.0, ((0, 8), (1, 4)))
    touched_ids = draw_touched_ids(jax.random.fold_in(key_list[10], 71), 0)
    touched_grads = scatter_about(key_list[9], (ROWS_ALL, D), 1.0, 5.0, ((0, 8), (1, 4)))
    return dict(hidden_acts=hidden_acts, out_grads=out_grads, errors=errors, factors=factors, whiten=whiten, momentum=momentum, master=master, table=table, touched_ids=touched_ids, touched_grads=touched_grads)


epsilon = 1e-06
momentum_decay = 0.9
learn_rate = 0.1
embed_rate = 0.25
clip_level = 0.03
highest = lax.Precision.HIGHEST

def corrected_block(pieces):
    grads_one, acts_one, error_one = pieces
    gradient = jnp.dot(grads_one.T, acts_one, preferred_element_type=jnp.float32)
    rounded = lax.optimization_barrier(gradient.astype(jnp.bfloat16))
    return rounded.astype(jnp.float32) + error_one

def reference(hidden_acts, out_grads, errors, factors, whiten, momentum, master, table, touched_ids, touched_grads):
    errors_list = []
    factor_list = []
    approx_list = []
    for which_layer in range(LAYERS):
        acts_layer = hidden_acts[which_layer].reshape(N_SHARD, TOK_DEV, FF)
        grads_layer = out_grads[which_layer].reshape(N_SHARD, TOK_DEV, D)
        corrected = lax.map(corrected_block, (grads_layer, acts_layer, errors[which_layer]))
        right_part = factors[which_layer]
        left_unit = None
        for power_round in range(ROUNDS):
            left_part = jnp.einsum('rf,ndf->rd', right_part, corrected, precision=highest)
            whitened = jnp.dot(whiten[which_layer, power_round].T, left_part, precision=highest)
            left_unit = whitened * lax.rsqrt(jnp.sum(whitened * whitened) / R + epsilon)
            right_part = jnp.einsum('rd,ndf->rf', left_unit, corrected, precision=highest) / N_SHARD
        approx = jnp.dot(left_unit.T, right_part, precision=highest)
        errors_list.append(corrected - approx[None])
        factor_list.append(right_part)
        approx_list.append(approx)
    approx_all = jnp.stack(approx_list)
    total_squares = jnp.sum(approx_all * approx_all)
    spread = jnp.sqrt(total_squares / (LAYERS * D * FF) + epsilon)
    clip_factor = jnp.minimum(1.0, clip_level / spread)
    new_momentum = momentum_decay * momentum + clip_factor * approx_all
    new_master = master - learn_rate * new_momentum
    new_weights = new_master.astype(jnp.bfloat16)
    table_grad = jnp.zeros((VOCAB, D), jnp.float32).at[touched_ids].add(touched_grads.astype(jnp.float32))
    new_table = (table.astype(jnp.float32) - embed_rate * table_grad).astype(jnp.bfloat16)
    return (jnp.stack(errors_list), jnp.stack(factor_list), new_momentum, new_master, new_weights, new_table)
```

```python
import functools

import jax
import jax.numpy as jnp
from jax import lax
from jax.experimental import pallas as pl
from jax.experimental.pallas import tpu as pltpu
from jax.sharding import PartitionSpec as P

ROUNDS = 2
LANES = 128
PIECE_ROWS = 32
CHUNKS = 5
TILE = 512
TABLE_ROWS = 1024

epsilon = 1e-06
momentum_decay = 0.9
learn_rate = 0.1
embed_rate = 0.25
clip_level = 0.03
highest = lax.Precision.HIGHEST
f32 = jnp.float32
bf16 = jnp.bfloat16
MESH = pl.DeviceIdType.MESH


def split(x):
    high = x.astype(bf16)
    low = (x - high.astype(f32)).astype(bf16)
    return high, low


def pieces(rank, width, count):
    rows = rank * (width // LANES) // count
    step = min(rows, rank)
    out = []
    for g in range(count):
        parts = []
        for at in range(0, rows, step):
            flat = g * rows + at
            parts.append((at, flat % rank, flat // rank * LANES, step))
        out.append(parts)
    return rows, out


def pack_rows(ids, touched, vocab, packed):
    owners, cap, _ = packed.shape
    count = touched.shape[0]
    owner = ids // vocab
    place = ids - owner * vocab
    owned = lax.broadcasted_iota(jnp.int32, (owners, count), 0) == owner
    before = lax.broadcasted_iota(jnp.int32, (count, count), 0) < lax.broadcasted_iota(
        jnp.int32, (count, count), 1
    )
    one = lambda mask: jnp.where(mask, 1.0, 0.0)
    ranks = jnp.dot(one(owned).astype(bf16), one(before).astype(bf16), preferred_element_type=f32)
    rank = jnp.sum(jnp.where(owned, ranks, 0.0), axis=0, keepdims=True)
    slot = owner * cap + rank.astype(jnp.int32)
    chosen = one(lax.broadcasted_iota(jnp.int32, (owners * cap, count), 0) == slot).astype(bf16)
    line = lax.broadcasted_iota(jnp.int32, (LANES, count), 0)
    coarse, fine = place // 128, place % 128
    notes = jnp.where(line == 0, coarse, jnp.where(line == 1, fine, jnp.where(line == 2, 1, 0)))
    sent = jnp.dot(chosen, touched, preferred_element_type=f32)
    sent_notes = jnp.dot(chosen, notes.astype(f32).T.astype(bf16), preferred_element_type=f32)
    width = touched.shape[1]
    for b in range(owners):
        packed[b, :, :width] = sent[b * cap : (b + 1) * cap].astype(bf16)
        packed[b, :, width:] = sent_notes[b * cap : (b + 1) * cap].astype(bf16)


def power_kernel(
    sizes,
    vocab,
    hidden_hbm,
    grads_hbm,
    errors_hbm,
    factors_hbm,
    whiten_hbm,
    momentum_hbm,
    master_hbm,
    table_hbm,
    ids_hbm,
    touched_hbm,
    corrected,
    left_ref,
    right_ref,
    total_ref,
    base_ref,
    momentum_ref,
    master_ref,
    table_ref,
    hidden,
    grads,
    errors,
    factors,
    whiten,
    ids,
    touched,
    high_ref,
    low_ref,
    lsend,
    lrecv,
    lgath,
    rsend0,
    rrecv0,
    rgath0,
    rsend1,
    rrecv1,
    rgath1,
    square,
    full,
    half,
    packed,
    found,
    lsem,
    rsem,
    qsem,
    tsem,
    bsem,
    msem,
    hsem,
    gsem,
):
    shards, tensors, sections = sizes
    rank, width = factors.shape
    depth = corrected.shape[0]
    tokens = hidden.shape[0]
    shard = lax.axis_index("shard")
    tensor = lax.axis_index("tensor")
    section = lax.axis_index("section")
    group = shards * tensors
    me = shard * tensors + tensor
    everyone = group * sections
    me_all = me * sections + section
    owners, cap, _ = packed.shape
    block = shard * sections + section

    def left_peer(k):
        index = lax.rem(me + k, group)
        return index, {"shard": index // tensors, "tensor": lax.rem(index, tensors)}

    def right_peer(k):
        index = lax.rem(shard + k, shards)
        return index, {"shard": index}

    def any_peer(k):
        index = lax.rem(me_all + k, everyone)
        pair = index // sections
        return index, {
            "shard": pair // tensors,
            "tensor": lax.rem(pair, tensors),
            "section": lax.rem(index, sections),
        }

    small = [
        (momentum_hbm, momentum_ref),
        (master_hbm, master_ref),
        (ids_hbm, ids),
        (touched_hbm, touched),
        (factors_hbm, factors),
        (whiten_hbm, whiten),
        (errors_hbm, errors),
        (table_hbm, table_ref),
    ]
    load = [pltpu.make_async_copy(src, dst, msem.at[i]) for i, (src, dst) in enumerate(small)]
    deep = tokens // CHUNKS
    acts = lambda k: pltpu.make_async_copy(
        hidden_hbm.at[pl.ds(k * deep, deep)], hidden.at[pl.ds(k * deep, deep)], hsem.at[k]
    )
    outs = lambda k: pltpu.make_async_copy(
        grads_hbm.at[pl.ds(k * deep, deep)], grads.at[pl.ds(k * deep, deep)], gsem.at[k]
    )
    for i in range(4):
        load[i].start()
    for k in range(CHUNKS):
        outs(k).start()
        acts(k).start()
    for i in range(4, 8):
        load[i].start()

    barrier = pltpu.get_barrier_semaphore()

    @pl.loop(1, everyone)
    def _(k):
        pl.semaphore_signal(barrier, inc=1, device_id=any_peer(k)[1], device_id_type=MESH)

    for i in range(4):
        load[i].wait()
    own_base = master_ref[...] - (learn_rate * momentum_decay) * momentum_ref[...]
    base_ref[shard] = own_base.astype(bf16)
    pack_rows(ids[...], touched[...], vocab, packed)
    pl.semaphore_wait(barrier, everyone - 1)

    def deliver(k):
        index = lax.rem(block + k, owners)
        return pltpu.make_async_remote_copy(
            src_ref=packed.at[index],
            dst_ref=found.at[block],
            send_sem=tsem.at[0, k],
            recv_sem=tsem.at[1, k],
            device_id={"shard": index // sections, "section": lax.rem(index, sections)},
            device_id_type=MESH,
        )

    rows_own = base_ref.shape[1]
    piece = min(PIECE_ROWS, rows_own)
    per_block = rows_own // piece
    steps = shards - 1
    n_pieces = steps * per_block
    taken = [0]

    def carry(way, q, receiving=False):
        step, part = q // per_block, q % per_block
        sign = 1 if way == 0 else -1
        at = shard - sign if receiving else shard
        index = lax.rem(at - sign * step + 2 * shards, shards)
        rows = pl.ds(part * piece, piece)
        return pltpu.make_async_remote_copy(
            src_ref=base_ref.at[index, rows],
            dst_ref=base_ref.at[index, rows],
            send_sem=bsem.at[way, 0, q],
            recv_sem=bsem.at[way, 1, q],
            device_id={"shard": lax.rem(shard + sign + shards, shards)},
            device_id_type=MESH,
        )

    def sends(way, q):
        step = q // per_block
        if way == 0:
            return jnp.logical_and(shard >= step, shard < shards - 1)
        return jnp.logical_and(shard < shards - step, shard > 0)

    def arrives(way, q):
        step = q // per_block
        return shard >= step + 1 if way == 0 else shard < shards - 1 - step

    def arrive(q):
        for way in (0, 1):

            @pl.when(arrives(way, q))
            def _():
                carry(way, q, True).wait_recv()

    def pump(count):
        for q in range(taken[0], min(n_pieces, taken[0] + count)):
            if q >= per_block:
                arrive(q - per_block)
            for way in (0, 1):

                @pl.when(sends(way, q))
                def _():
                    carry(way, q).start()

            taken[0] = q + 1

    slots = [max(1, (n_pieces * share + 23) // 24) for share in PACE]
    slot = [0]

    def next_slot():
        pump(slots[slot[0]])
        slot[0] += 1

    @pl.loop(1, owners)
    def _(k):
        deliver(k).start()

    next_slot()

    tiles = depth // TILE
    for k in range(CHUNKS):
        outs(k).wait()
        acts(k).wait()
        at = slice(k * deep, (k + 1) * deep)
        for j in range(tiles):
            rows = slice(j * TILE, (j + 1) * TILE)
            part = lax.dot_general(
                grads[at, rows], hidden[at, :], (((0,), (0,)), ((), ())), preferred_element_type=f32
            )
            if k == 0:
                corrected[rows, :] = part
            elif k < CHUNKS - 1:
                corrected[rows, :] += part
            else:
                if j == 0:
                    load[6].wait()
                    load[4].wait()
                    load[5].wait()
                summed = (corrected[rows, :] + part).astype(bf16).astype(f32) + errors[rows, :]
                corrected[rows, :] = summed
                high, low = split(summed)
                high_ref[rows, :] = high
                low_ref[rows, :] = low
        if k < CHUNKS - 1:
            next_slot()

    def table_part(i):
        count = min(TABLE_ROWS, table_ref.shape[0])
        at = slice(i * count, (i + 1) * count)
        cols = table_ref.shape[1]
        rows = found[...].reshape(owners * cap, found.shape[2])
        notes = rows[:, cols:].astype(f32).T
        place = notes[0:1] * 128.0 + notes[1:2] - (1.0 - notes[2:3])
        index = place.astype(jnp.int32) - i * count
        places = lax.broadcasted_iota(jnp.int32, (count, index.shape[1]), 0)
        chosen = jnp.where(places == index, 1.0, 0.0).astype(bf16)
        table_grad = jnp.dot(chosen, rows[:, :cols], preferred_element_type=f32)
        table_ref[at, :] = (table_ref[at, :].astype(f32) - embed_rate * table_grad).astype(bf16)

    table_parts = max(1, table_ref.shape[0] // TABLE_ROWS)

    def delivered():
        @pl.loop(1, owners)
        def _(k):
            deliver(k).wait()

        found[block] = packed[block]
        load[7].wait()

    def start(count, copy):
        if count <= 16:
            for k in range(1, count):
                copy(k).start()
        else:

            @pl.loop(1, count)
            def _(k):
                copy(k).start()

    def finish(count, copy):
        @pl.loop(1, count)
        def _(k):
            copy(k).wait()

    def all_reduce(value, count, own, peer, send, recv, gath, sems, after, meanwhile, into):
        rows, cuts = pieces(value.shape[0], value.shape[1], count)
        wire = send.dtype
        value = value.astype(wire)
        for g in range(count):
            for at, row, col, step in cuts[g]:
                send[g, at : at + step, :] = value[row : row + step, col : col + LANES]

        def scatter(k):
            index, there = peer(k)
            return pltpu.make_async_remote_copy(
                src_ref=send.at[index],
                dst_ref=recv.at[k],
                send_sem=sems.at[0, k],
                recv_sem=sems.at[1, k],
                device_id=there,
                device_id_type=MESH,
            )

        start(count, scatter)
        next_slot()
        meanwhile[0]()
        finish(count, scatter)
        total = send[own].astype(f32)
        for k in range(1, count):
            total = total + recv[k].astype(f32)
        total = after(total)
        gath[own] = total.astype(gath.dtype)

        def gather(k):
            _, there = peer(k)
            return pltpu.make_async_remote_copy(
                src_ref=gath.at[own],
                dst_ref=gath.at[own],
                send_sem=sems.at[2, k],
                recv_sem=sems.at[3, k],
                device_id=there,
                device_id_type=MESH,
            )

        start(count, gather)
        meanwhile[1](total)
        next_slot()
        meanwhile[2]()
        finish(count, gather)
        for g in range(count):
            for at, row, col, step in cuts[g]:
                into[row : row + step, col : col + LANES] = gath[g, at : at + step, :]
        return into[...]

    def times(x, dims, x_low, c_low):
        if x.dtype == bf16:
            return lax.dot_general(x, high_ref[...], (dims, ((), ())), preferred_element_type=f32)
        high, low = split(x)
        both = jnp.concatenate([high, low], axis=0)
        first = lax.dot_general(both, high_ref[...], (dims, ((), ())), preferred_element_type=f32)
        out = first[rank:]
        if c_low:
            out = out + lax.dot_general(high, low_ref[...], (dims, ((), ())), preferred_element_type=f32)
        return first[:rank] + out

    last = (((1,), (1,)), ((), ()))
    idle = lambda *_: None
    same = lambda x: x

    def share(k):
        _, there = any_peer(k)
        return pltpu.make_async_remote_copy(
            src_ref=square.at[0],
            dst_ref=square.at[k],
            send_sem=qsem.at[0, k],
            recv_sem=qsem.at[1, k],
            device_id=there,
            device_id_type=MESH,
        )

    table_at = [0]

    def some_table():
        if table_at[0] == 0:
            delivered()
        if table_at[0] < table_parts:
            table_part(table_at[0])
        table_at[0] += 1

    right = factors[...]
    for turn in range(ROUNDS):
        final = turn == ROUNDS - 1
        left_part = times(right, ((1,), (1,)), turn == 0, turn == 0)
        busy = some_table if turn > 0 else idle
        left = all_reduce(
            left_part, group, me, left_peer, lsend.at[turn], lrecv.at[turn], lgath.at[turn], lsem.at[turn],
            same, (busy, idle, busy), full,
        )
        whitened = lax.dot_general(
            whiten[turn], left, (((0,), (0,)), ((), ())), precision=highest, preferred_element_type=f32
        )
        scale = lax.rsqrt(jnp.sum(whitened * whitened) / rank + epsilon)
        right_part = times(whitened, ((1,), (0,)), True, final)
        rsend, rrecv, rgath = (rsend1, rrecv1, rgath1) if final else (rsend0, rrecv0, rgath0)
        into = half if rgath.dtype == bf16 else full
        if not final:
            right = all_reduce(
                right_part, shards, shard, right_peer, rsend, rrecv, rgath, rsem.at[turn],
                lambda x: x * (scale * (1.0 / shards)), (some_table, idle, some_table), into,
            )
            continue
        left_unit = whitened * scale
        kept = []

        def prepare():
            left_high = left_unit.astype(bf16).astype(f32)
            stacked = jnp.concatenate([left_high, left_unit - left_high, left_high], axis=0)
            left_ref[...] = stacked.T.astype(bf16)
            kept.append(lax.dot_general(left_unit, left_unit, last, precision=highest, preferred_element_type=f32))

        def announce(gram_right, weight):
            amount = jnp.sum(kept[0] * gram_right) * weight
            square[0] = jnp.full(square.shape[1:], amount, f32)
            start(everyone, share)

        def own_squares(total):
            if total.shape[0] % rank:
                return
            gram = None
            for at in range(0, total.shape[0], rank):
                cols = total[at : at + rank]
                term = lax.dot_general(cols, cols, last, precision=highest, preferred_element_type=f32)
                gram = term if gram is None else gram + term
            announce(gram, 1.0)

        right = all_reduce(
            right_part, shards, shard, right_peer, rsend, rrecv, rgath, rsem.at[turn],
            lambda x: x * (scale * (1.0 / shards)), (prepare, own_squares, idle), into,
        )
        if rgath.shape[1] % rank:
            gram = lax.dot_general(right, right, last, precision=highest, preferred_element_type=f32)
            announce(gram, 1.0 / shards)

    right_ref[...] = right
    while table_at[0] < table_parts:
        some_table()
    pump(n_pieces)
    for q in range(max(0, n_pieces - per_block), n_pieces):
        arrive(q)
    finish(everyone, share)
    total_ref[...] = jnp.broadcast_to(jnp.sum(square[...], axis=0), total_ref.shape)
    for q in range(n_pieces):
        for way in (0, 1):

            @pl.when(sends(way, q))
            def _():
                carry(way, q).wait_send()


PACE = (5, 1, 1, 1, 1, 1, 2, 2, 2, 2, 2, 2, 2)


def run_power(sizes, vocab, hidden, grads, errors, factors, whiten, momentum, master, table, ids, touched):
    shards, tensors, sections = sizes
    rank, width = factors.shape
    tokens, depth = grads.shape
    rows_own = momentum.shape[0]
    owners = shards * sections
    cap = 2 * touched.shape[0] // owners
    packed = (owners, cap, touched.shape[1] + LANES)
    group = shards * tensors
    everyone = group * sections
    left_rows = rank * (depth // LANES) // group
    right_rows = rank * (width // LANES) // shards
    narrow = lambda rows: bf16 if rows % 16 == 0 else f32
    per_block = rows_own // min(PIECE_ROWS, rows_own)
    hbm = pl.BlockSpec(memory_space=pltpu.HBM)
    vmem = pl.BlockSpec(memory_space=pltpu.VMEM)
    return pl.pallas_call(
        functools.partial(power_kernel, sizes, vocab),
        out_shape=(
            jax.ShapeDtypeStruct((depth, width), f32),
            jax.ShapeDtypeStruct((depth, 3 * rank), bf16),
            jax.ShapeDtypeStruct((rank, width), f32),
            jax.ShapeDtypeStruct((8, LANES), f32),
            jax.ShapeDtypeStruct((shards, rows_own, width), bf16),
            jax.ShapeDtypeStruct(momentum.shape, f32),
            jax.ShapeDtypeStruct(master.shape, f32),
            jax.ShapeDtypeStruct(table.shape, bf16),
        ),
        in_specs=[hbm] * 10,
        out_specs=(vmem,) * 8,
        scratch_shapes=[
            pltpu.VMEM(hidden.shape, bf16),
            pltpu.VMEM(grads.shape, bf16),
            pltpu.VMEM(errors.shape, f32),
            pltpu.VMEM(factors.shape, f32),
            pltpu.VMEM(whiten.shape, f32),
            pltpu.VMEM(ids.shape, jnp.int32),
            pltpu.VMEM(touched.shape, bf16),
            pltpu.VMEM((depth, width), bf16),
            pltpu.VMEM((depth, width), bf16),
            pltpu.VMEM((ROUNDS, group, left_rows, LANES), narrow(left_rows)),
            pltpu.VMEM((ROUNDS, group, left_rows, LANES), narrow(left_rows)),
            pltpu.VMEM((ROUNDS, group, left_rows, LANES), f32),
            pltpu.VMEM((shards, right_rows, LANES), narrow(right_rows)),
            pltpu.VMEM((shards, right_rows, LANES), narrow(right_rows)),
            pltpu.VMEM((shards, right_rows, LANES), narrow(right_rows)),
            pltpu.VMEM((shards, right_rows, LANES), f32),
            pltpu.VMEM((shards, right_rows, LANES), f32),
            pltpu.VMEM((shards, right_rows, LANES), f32),
            pltpu.VMEM((everyone, 1, LANES), f32),
            pltpu.VMEM((rank, max(depth, width)), f32),
            pltpu.VMEM((rank, max(depth, width)), bf16),
            pltpu.VMEM(packed, bf16),
            pltpu.VMEM(packed, bf16),
            pltpu.SemaphoreType.DMA((ROUNDS, 4, group)),
            pltpu.SemaphoreType.DMA((ROUNDS, 4, shards)),
            pltpu.SemaphoreType.DMA((2, everyone)),
            pltpu.SemaphoreType.DMA((2, owners)),
            pltpu.SemaphoreType.DMA((2, 2, (shards - 1) * per_block)),
            pltpu.SemaphoreType.DMA((8,)),
            pltpu.SemaphoreType.DMA((CHUNKS,)),
            pltpu.SemaphoreType.DMA((CHUNKS,)),
        ],
        compiler_params=pltpu.CompilerParams(
            collective_id=0, has_side_effects=True, vmem_limit_bytes=36 * 2**20
        ),
        cost_estimate=pl.CostEstimate(flops=6 * 10**9, bytes_accessed=20 * 10**6, transcendentals=0),
        name="power_rounds",
    )(hidden, grads, errors, factors, whiten, momentum, master, table, ids, touched)


def update_kernel(
    shards,
    entries,
    corrected,
    left_ref,
    right_ref,
    total_ref,
    base_ref,
    momentum_ref,
    master_ref,
    table_ref,
    errors_out,
    factors_out,
    momentum_out,
    master_out,
    weights_out,
    table_out,
    errors_new,
    momentum_new,
    master_new,
    weights_new,
    esem,
    wsem,
    msem,
):
    shard = lax.axis_index("shard")
    rows = momentum_ref.shape[0]
    writes = [
        pltpu.make_async_copy(table_ref, table_out, msem.at[0]),
        pltpu.make_async_copy(right_ref, factors_out, msem.at[1]),
    ]
    for write in writes:
        write.start()
    right = right_ref[...]
    high, low = split(right)
    stacked = jnp.concatenate([high, high, low], axis=0)
    spread = jnp.sqrt(total_ref[0:1, 0:1] / entries + epsilon)
    clip = jnp.minimum(1.0, clip_level / spread)
    for i in range(shards):
        at = pl.ds(i * rows, rows)
        approx = jnp.dot(left_ref[at, :], stacked, preferred_element_type=f32)
        errors_new[at, :] = corrected[at, :] - approx
        write = pltpu.make_async_copy(errors_new.at[at], errors_out.at[at], esem.at[i])
        write.start()
        writes.append(write)
        clipped = clip * approx

        @pl.when(shard == i)
        def _():
            moved = momentum_decay * momentum_ref[...] + clipped
            stepped = master_ref[...] - learn_rate * moved
            momentum_new[...] = moved
            master_new[...] = stepped
            weights_new[at, :] = stepped.astype(bf16)

        @pl.when(shard != i)
        def _():
            weights_new[at, :] = (base_ref[i].astype(f32) - learn_rate * clipped).astype(bf16)

        write = pltpu.make_async_copy(weights_new.at[at], weights_out.at[at], wsem.at[i])
        write.start()
        writes.append(write)
    for write in (
        pltpu.make_async_copy(momentum_new, momentum_out, msem.at[2]),
        pltpu.make_async_copy(master_new, master_out, msem.at[3]),
    ):
        write.start()
        writes.append(write)
    for write in writes:
        write.wait()


def run_update(shards, entries, corrected, left, right, total, base, momentum, master, table):
    depth, width = corrected.shape
    hbm = pl.BlockSpec(memory_space=pltpu.HBM)
    vmem = pl.BlockSpec(memory_space=pltpu.VMEM)
    return pl.pallas_call(
        functools.partial(update_kernel, shards, entries),
        out_shape=(
            jax.ShapeDtypeStruct((depth, width), f32),
            jax.ShapeDtypeStruct(right.shape, f32),
            jax.ShapeDtypeStruct(momentum.shape, f32),
            jax.ShapeDtypeStruct(master.shape, f32),
            jax.ShapeDtypeStruct((depth, width), bf16),
            jax.ShapeDtypeStruct(table.shape, bf16),
        ),
        in_specs=[vmem] * 8,
        out_specs=(hbm,) * 6,
        scratch_shapes=[
            pltpu.VMEM((depth, width), f32),
            pltpu.VMEM(momentum.shape, f32),
            pltpu.VMEM(master.shape, f32),
            pltpu.VMEM((depth, width), bf16),
            pltpu.SemaphoreType.DMA((shards,)),
            pltpu.SemaphoreType.DMA((shards,)),
            pltpu.SemaphoreType.DMA((4,)),
        ],
        compiler_params=pltpu.CompilerParams(vmem_limit_bytes=30 * 2**20),
        name="apply_update",
    )(corrected, left, right, total, base, momentum, master, table)


def solution(mesh):
    shards, tensors, sections = (mesh.shape[a] for a in ("shard", "tensor", "section"))
    sizes = (shards, tensors, sections)

    def on_device(
        hidden_acts, out_grads, errors, factors, whiten, momentum, master, table, touched_ids, touched_grads
    ):
        power = run_power(
            sizes, table.shape[0], hidden_acts[0], out_grads[0], errors[0, 0], factors[0], whiten[0],
            momentum[0], master[0], table, touched_ids[None], touched_grads,
        )
        depth, width = errors.shape[2:]
        entries = sections * depth * width * tensors
        new_errors, new_factors, new_momentum, new_master, new_weights, new_table = run_update(
            shards, entries, *power
        )
        return (
            new_errors[None, None],
            new_factors[None],
            new_momentum[None],
            new_master[None],
            new_weights[None],
            new_table,
        )

    in_specs = (
        P("section", "shard", "tensor"),
        P("section", "shard", None),
        P("section", "shard", None, "tensor"),
        P("section", None, "tensor"),
        P("section", None, None, None),
        P("section", "shard", "tensor"),
        P("section", "shard", "tensor"),
        P(("shard", "section"), "tensor"),
        P(("shard", "section")),
        P(("shard", "section"), "tensor"),
    )
    out_specs = (
        P("section", "shard", None, "tensor"),
        P("section", None, "tensor"),
        P("section", "shard", "tensor"),
        P("section", "shard", "tensor"),
        P("section", None, "tensor"),
        P(("shard", "section"), "tensor"),
    )
    return jax.shard_map(on_device, mesh=mesh, in_specs=in_specs, out_specs=out_specs, check_vma=False)
```

```python
import functools

import jax
import jax.numpy as jnp
from jax import lax
from jax.experimental import pallas as pl
from jax.experimental.pallas import tpu as pltpu
from jax.sharding import PartitionSpec as P

ROUNDS = 2
LANES = 128
PIECE_ROWS = 32
CHUNKS = 5
TILE = 512
TABLE_ROWS = 1024

epsilon = 1e-06
momentum_decay = 0.9
learn_rate = 0.1
embed_rate = 0.25
clip_level = 0.03
highest = lax.Precision.HIGHEST
f32 = jnp.float32
bf16 = jnp.bfloat16
MESH = pl.DeviceIdType.MESH


def split(x):
    high = x.astype(bf16)
    low = (x - high.astype(f32)).astype(bf16)
    return high, low


def pieces(rank, width, count):
    rows = rank * (width // LANES) // count
    step = min(rows, rank)
    out = []
    for g in range(count):
        parts = []
        for at in range(0, rows, step):
            flat = g * rows + at
            parts.append((at, flat % rank, flat // rank * LANES, step))
        out.append(parts)
    return rows, out


def pack_rows(ids, touched, vocab, packed):
    owners, cap, _ = packed.shape
    count = touched.shape[0]
    owner = ids // vocab
    place = ids - owner * vocab
    owned = lax.broadcasted_iota(jnp.int32, (owners, count), 0) == owner
    before = lax.broadcasted_iota(jnp.int32, (count, count), 0) < lax.broadcasted_iota(
        jnp.int32, (count, count), 1
    )
    one = lambda mask: jnp.where(mask, 1.0, 0.0)
    ranks = jnp.dot(one(owned).astype(bf16), one(before).astype(bf16), preferred_element_type=f32)
    rank = jnp.sum(jnp.where(owned, ranks, 0.0), axis=0, keepdims=True)
    slot = owner * cap + rank.astype(jnp.int32)
    chosen = one(lax.broadcasted_iota(jnp.int32, (owners * cap, count), 0) == slot).astype(bf16)
    line = lax.broadcasted_iota(jnp.int32, (LANES, count), 0)
    coarse, fine = place // 128, place % 128
    notes = jnp.where(line == 0, coarse, jnp.where(line == 1, fine, jnp.where(line == 2, 1, 0)))
    sent = jnp.dot(chosen, touched, preferred_element_type=f32)
    sent_notes = jnp.dot(chosen, notes.astype(f32).T.astype(bf16), preferred_element_type=f32)
    width = touched.shape[1]
    for b in range(owners):
        packed[b, :, :width] = sent[b * cap : (b + 1) * cap].astype(bf16)
        packed[b, :, width:] = sent_notes[b * cap : (b + 1) * cap].astype(bf16)


def power_kernel(
    sizes,
    vocab,
    hidden_hbm,
    grads_hbm,
    errors_hbm,
    factors_hbm,
    whiten_hbm,
    momentum_hbm,
    master_hbm,
    table_hbm,
    ids_hbm,
    touched_hbm,
    corrected,
    left_ref,
    right_ref,
    total_ref,
    base_ref,
    momentum_ref,
    master_ref,
    table_ref,
    hidden,
    grads,
    errors,
    factors,
    whiten,
    ids,
    touched,
    high_ref,
    low_ref,
    lsend,
    lrecv,
    lgath,
    rsend0,
    rrecv0,
    rgath0,
    rsend1,
    rrecv1,
    rgath1,
    square,
    full,
    half,
    packed,
    found,
    lsem,
    rsem,
    qsem,
    tsem,
    bsem,
    msem,
    hsem,
    gsem,
):
    shards, tensors, sections = sizes
    rank, width = factors.shape
    depth = corrected.shape[0]
    tokens = hidden.shape[0]
    shard = lax.axis_index("shard")
    tensor = lax.axis_index("tensor")
    section = lax.axis_index("section")
    group = shards * tensors
    me = shard * tensors + tensor
    everyone = group * sections
    me_all = me * sections + section
    owners, cap, _ = packed.shape
    block = shard * sections + section

    def left_peer(k):
        index = lax.rem(me + k, group)
        return index, {"shard": index // tensors, "tensor": lax.rem(index, tensors)}

    def right_peer(k):
        index = lax.rem(shard + k, shards)
        return index, {"shard": index}

    def any_peer(k):
        index = lax.rem(me_all + k, everyone)
        pair = index // sections
        return index, {
            "shard": pair // tensors,
            "tensor": lax.rem(pair, tensors),
            "section": lax.rem(index, sections),
        }

    small = [
        (momentum_hbm, momentum_ref),
        (master_hbm, master_ref),
        (ids_hbm, ids),
        (touched_hbm, touched),
        (factors_hbm, factors),
        (whiten_hbm, whiten),
        (errors_hbm, errors),
        (table_hbm, table_ref),
    ]
    load = [pltpu.make_async_copy(src, dst, msem.at[i]) for i, (src, dst) in enumerate(small)]
    deep = tokens // CHUNKS
    acts = lambda k: pltpu.make_async_copy(
        hidden_hbm.at[pl.ds(k * deep, deep)], hidden.at[pl.ds(k * deep, deep)], hsem.at[k]
    )
    outs = lambda k: pltpu.make_async_copy(
        grads_hbm.at[pl.ds(k * deep, deep)], grads.at[pl.ds(k * deep, deep)], gsem.at[k]
    )
    for k in range(CHUNKS):
        outs(k).start()
        acts(k).start()
        if k == 0:
            for i in range(4):
                load[i].start()
    for i in range(4, 8):
        load[i].start()

    barrier = pltpu.get_barrier_semaphore()

    @pl.loop(1, everyone)
    def _(k):
        pl.semaphore_signal(barrier, inc=1, device_id=any_peer(k)[1], device_id_type=MESH)

    def deliver(k):
        index = lax.rem(block + k, owners)
        return pltpu.make_async_remote_copy(
            src_ref=packed.at[index],
            dst_ref=found.at[block],
            send_sem=tsem.at[0, k],
            recv_sem=tsem.at[1, k],
            device_id={"shard": index // sections, "section": lax.rem(index, sections)},
            device_id_type=MESH,
        )

    rows_own = base_ref.shape[1]
    piece = min(PIECE_ROWS, rows_own)
    per_block = rows_own // piece
    steps = shards - 1
    n_pieces = steps * per_block
    taken = [0]

    def carry(way, q, receiving=False):
        step, part = q // per_block, q % per_block
        sign = 1 if way == 0 else -1
        at = shard - sign if receiving else shard
        index = lax.rem(at - sign * step + 2 * shards, shards)
        rows = pl.ds(part * piece, piece)
        return pltpu.make_async_remote_copy(
            src_ref=base_ref.at[index, rows],
            dst_ref=base_ref.at[index, rows],
            send_sem=bsem.at[way, 0, q],
            recv_sem=bsem.at[way, 1, q],
            device_id={"shard": lax.rem(shard + sign + shards, shards)},
            device_id_type=MESH,
        )

    def sends(way, q):
        step = q // per_block
        if way == 0:
            return jnp.logical_and(shard >= step, shard < shards - 1)
        return jnp.logical_and(shard < shards - step, shard > 0)

    def arrives(way, q):
        step = q // per_block
        return shard >= step + 1 if way == 0 else shard < shards - 1 - step

    def arrive(q):
        for way in (0, 1):

            @pl.when(arrives(way, q))
            def _():
                carry(way, q, True).wait_recv()

    def pump(count):
        for q in range(taken[0], min(n_pieces, taken[0] + count)):
            if q >= per_block:
                arrive(q - per_block)
            for way in (0, 1):

                @pl.when(sends(way, q))
                def _():
                    carry(way, q).start()

            taken[0] = q + 1

    slots = [max(1, (n_pieces * share + 23) // 24) for share in PACE]
    slot = [0]

    def next_slot():
        pump(slots[slot[0]])
        slot[0] += 1

    tiles = depth // TILE
    for k in range(CHUNKS):
        outs(k).wait()
        acts(k).wait()
        at = slice(k * deep, (k + 1) * deep)
        for j in range(tiles):
            rows = slice(j * TILE, (j + 1) * TILE)
            part = lax.dot_general(
                grads[at, rows], hidden[at, :], (((0,), (0,)), ((), ())), preferred_element_type=f32
            )
            if k == 0:
                corrected[rows, :] = part
            elif k < CHUNKS - 1:
                corrected[rows, :] += part
            else:
                if j == 0:
                    load[6].wait()
                    load[4].wait()
                    load[5].wait()
                summed = (corrected[rows, :] + part).astype(bf16).astype(f32) + errors[rows, :]
                corrected[rows, :] = summed
                high, low = split(summed)
                high_ref[rows, :] = high
                low_ref[rows, :] = low
        if k == 0:
            load[0].wait()
            load[1].wait()
            own_base = master_ref[...] - (learn_rate * momentum_decay) * momentum_ref[...]
            base_ref[shard] = own_base.astype(bf16)
            pl.semaphore_wait(barrier, everyone - 1)
            next_slot()
        elif k == 1:
            load[2].wait()
            load[3].wait()
            pack_rows(ids[...], touched[...], vocab, packed)

            @pl.loop(1, owners)
            def _(k):
                deliver(k).start()

        if k < CHUNKS - 1:
            next_slot()

    def table_part(i):
        count = min(TABLE_ROWS, table_ref.shape[0])
        at = slice(i * count, (i + 1) * count)
        cols = table_ref.shape[1]
        rows = found[...].reshape(owners * cap, found.shape[2])
        notes = rows[:, cols:].astype(f32).T
        place = notes[0:1] * 128.0 + notes[1:2] - (1.0 - notes[2:3])
        index = place.astype(jnp.int32) - i * count
        places = lax.broadcasted_iota(jnp.int32, (count, index.shape[1]), 0)
        chosen = jnp.where(places == index, 1.0, 0.0).astype(bf16)
        table_grad = jnp.dot(chosen, rows[:, :cols], preferred_element_type=f32)
        table_ref[at, :] = (table_ref[at, :].astype(f32) - embed_rate * table_grad).astype(bf16)

    table_parts = max(1, table_ref.shape[0] // TABLE_ROWS)

    def delivered():
        @pl.loop(1, owners)
        def _(k):
            deliver(k).wait()

        found[block] = packed[block]
        load[7].wait()

    def start(count, copy):
        if count <= 16:
            for k in range(1, count):
                copy(k).start()
        else:

            @pl.loop(1, count)
            def _(k):
                copy(k).start()

    def finish(count, copy):
        @pl.loop(1, count)
        def _(k):
            copy(k).wait()

    def all_reduce(value, count, own, peer, send, recv, gath, sems, after, meanwhile, into):
        rows, cuts = pieces(value.shape[0], value.shape[1], count)
        wire = send.dtype
        value = value.astype(wire)
        for g in range(count):
            for at, row, col, step in cuts[g]:
                send[g, at : at + step, :] = value[row : row + step, col : col + LANES]

        def scatter(k):
            index, there = peer(k)
            return pltpu.make_async_remote_copy(
                src_ref=send.at[index],
                dst_ref=recv.at[k],
                send_sem=sems.at[0, k],
                recv_sem=sems.at[1, k],
                device_id=there,
                device_id_type=MESH,
            )

        start(count, scatter)
        next_slot()
        meanwhile[0]()
        finish(count, scatter)
        total = send[own].astype(f32)
        for k in range(1, count):
            total = total + recv[k].astype(f32)
        total = after(total)
        gath[own] = total.astype(gath.dtype)

        def gather(k):
            _, there = peer(k)
            return pltpu.make_async_remote_copy(
                src_ref=gath.at[own],
                dst_ref=gath.at[own],
                send_sem=sems.at[2, k],
                recv_sem=sems.at[3, k],
                device_id=there,
                device_id_type=MESH,
            )

        start(count, gather)
        meanwhile[1](total)
        next_slot()
        meanwhile[2]()
        finish(count, gather)
        for g in range(count):
            for at, row, col, step in cuts[g]:
                into[row : row + step, col : col + LANES] = gath[g, at : at + step, :]
        return into[...]

    def times(x, dims, x_low, c_low):
        if x.dtype == bf16:
            return lax.dot_general(x, high_ref[...], (dims, ((), ())), preferred_element_type=f32)
        high, low = split(x)
        both = jnp.concatenate([high, low], axis=0)
        first = lax.dot_general(both, high_ref[...], (dims, ((), ())), preferred_element_type=f32)
        out = first[rank:]
        if c_low:
            out = out + lax.dot_general(high, low_ref[...], (dims, ((), ())), preferred_element_type=f32)
        return first[:rank] + out

    last = (((1,), (1,)), ((), ()))
    idle = lambda *_: None
    same = lambda x: x

    def share(k):
        _, there = any_peer(k)
        return pltpu.make_async_remote_copy(
            src_ref=square.at[0],
            dst_ref=square.at[k],
            send_sem=qsem.at[0, k],
            recv_sem=qsem.at[1, k],
            device_id=there,
            device_id_type=MESH,
        )

    table_at = [0]

    def some_table():
        if table_at[0] == 0:
            delivered()
        if table_at[0] < table_parts:
            table_part(table_at[0])
        table_at[0] += 1

    right = factors[...]
    for turn in range(ROUNDS):
        final = turn == ROUNDS - 1
        left_part = times(right, ((1,), (1,)), turn == 0, turn == 0)
        busy = some_table if turn > 0 else idle
        left = all_reduce(
            left_part, group, me, left_peer, lsend.at[turn], lrecv.at[turn], lgath.at[turn], lsem.at[turn],
            same, (busy, idle, busy), half if lgath.dtype == bf16 else full,
        )
        whitened = lax.dot_general(
            whiten[turn], left.astype(f32), (((0,), (0,)), ((), ())), precision=highest, preferred_element_type=f32
        )
        scale = lax.rsqrt(jnp.sum(whitened * whitened) / rank + epsilon)
        right_part = times(whitened, ((1,), (0,)), True, final)
        rsend, rrecv, rgath = (rsend1, rrecv1, rgath1) if final else (rsend0, rrecv0, rgath0)
        into = half if rgath.dtype == bf16 else full
        if not final:
            right = all_reduce(
                right_part, shards, shard, right_peer, rsend, rrecv, rgath, rsem.at[turn],
                lambda x: x * (scale * (1.0 / shards)), (some_table, idle, some_table), into,
            )
            continue
        left_unit = whitened * scale
        kept = []

        def prepare():
            left_high = left_unit.astype(bf16).astype(f32)
            stacked = jnp.concatenate([left_high, left_unit - left_high, left_high], axis=0)
            left_ref[...] = stacked.T.astype(bf16)
            kept.append(lax.dot_general(left_unit, left_unit, last, precision=highest, preferred_element_type=f32))

        def announce(gram_right, weight):
            amount = jnp.sum(kept[0] * gram_right) * weight
            square[0] = jnp.full(square.shape[1:], amount, f32)
            start(everyone, share)

        def own_squares(total):
            if total.shape[0] % rank:
                return
            gram = None
            for at in range(0, total.shape[0], rank):
                cols = total[at : at + rank]
                term = lax.dot_general(cols, cols, last, precision=highest, preferred_element_type=f32)
                gram = term if gram is None else gram + term
            announce(gram, 1.0)

        right = all_reduce(
            right_part, shards, shard, right_peer, rsend, rrecv, rgath, rsem.at[turn],
            lambda x: x * (scale * (1.0 / shards)), (prepare, own_squares, idle), into,
        )
        if rgath.shape[1] % rank:
            gram = lax.dot_general(right, right, last, precision=highest, preferred_element_type=f32)
            announce(gram, 1.0 / shards)

    right_ref[...] = right
    while table_at[0] < table_parts:
        some_table()
    pump(n_pieces)
    for q in range(max(0, n_pieces - per_block), n_pieces):
        arrive(q)
    finish(everyone, share)
    total_ref[...] = jnp.broadcast_to(jnp.sum(square[...], axis=0), total_ref.shape)
    for q in range(n_pieces):
        for way in (0, 1):

            @pl.when(sends(way, q))
            def _():
                carry(way, q).wait_send()


PACE = (5, 1, 1, 1, 1, 1, 2, 2, 2, 2, 2, 2, 2)


def run_power(sizes, vocab, hidden, grads, errors, factors, whiten, momentum, master, table, ids, touched):
    shards, tensors, sections = sizes
    rank, width = factors.shape
    tokens, depth = grads.shape
    rows_own = momentum.shape[0]
    owners = shards * sections
    cap = 2 * touched.shape[0] // owners
    packed = (owners, cap, touched.shape[1] + LANES)
    group = shards * tensors
    everyone = group * sections
    left_rows = rank * (depth // LANES) // group
    right_rows = rank * (width // LANES) // shards
    operands = (hidden, grads, errors, factors, whiten, momentum, master, table, ids, touched)
    narrow = lambda rows: bf16 if rows % 16 == 0 else f32
    per_block = rows_own // min(PIECE_ROWS, rows_own)
    hbm = pl.BlockSpec(memory_space=pltpu.HBM)
    vmem = pl.BlockSpec(memory_space=pltpu.VMEM)
    return pl.pallas_call(
        functools.partial(power_kernel, sizes, vocab),
        out_shape=(
            jax.ShapeDtypeStruct((depth, width), f32),
            jax.ShapeDtypeStruct((depth, 3 * rank), bf16),
            jax.ShapeDtypeStruct((rank, width), f32),
            jax.ShapeDtypeStruct((8, LANES), f32),
            jax.ShapeDtypeStruct((shards, rows_own, width), bf16),
            jax.ShapeDtypeStruct(momentum.shape, f32),
            jax.ShapeDtypeStruct(master.shape, f32),
            jax.ShapeDtypeStruct(table.shape, bf16),
        ),
        in_specs=[hbm] * 10,
        out_specs=(vmem,) * 8,
        scratch_shapes=[
            pltpu.VMEM(hidden.shape, bf16),
            pltpu.VMEM(grads.shape, bf16),
            pltpu.VMEM(errors.shape, f32),
            pltpu.VMEM(factors.shape, f32),
            pltpu.VMEM(whiten.shape, f32),
            pltpu.VMEM(ids.shape, jnp.int32),
            pltpu.VMEM(touched.shape, bf16),
            pltpu.VMEM((depth, width), bf16),
            pltpu.VMEM((depth, width), bf16),
            pltpu.VMEM((ROUNDS, group, left_rows, LANES), narrow(left_rows)),
            pltpu.VMEM((ROUNDS, group, left_rows, LANES), narrow(left_rows)),
            pltpu.VMEM((ROUNDS, group, left_rows, LANES), narrow(left_rows)),
            pltpu.VMEM((shards, right_rows, LANES), narrow(right_rows)),
            pltpu.VMEM((shards, right_rows, LANES), narrow(right_rows)),
            pltpu.VMEM((shards, right_rows, LANES), narrow(right_rows)),
            pltpu.VMEM((shards, right_rows, LANES), f32),
            pltpu.VMEM((shards, right_rows, LANES), f32),
            pltpu.VMEM((shards, right_rows, LANES), f32),
            pltpu.VMEM((everyone, 1, LANES), f32),
            pltpu.VMEM((rank, max(depth, width)), f32),
            pltpu.VMEM((rank, max(depth, width)), bf16),
            pltpu.VMEM(packed, bf16),
            pltpu.VMEM(packed, bf16),
            pltpu.SemaphoreType.DMA((ROUNDS, 4, group)),
            pltpu.SemaphoreType.DMA((ROUNDS, 4, shards)),
            pltpu.SemaphoreType.DMA((2, everyone)),
            pltpu.SemaphoreType.DMA((2, owners)),
            pltpu.SemaphoreType.DMA((2, 2, (shards - 1) * per_block)),
            pltpu.SemaphoreType.DMA((8,)),
            pltpu.SemaphoreType.DMA((CHUNKS,)),
            pltpu.SemaphoreType.DMA((CHUNKS,)),
        ],
        compiler_params=pltpu.CompilerParams(
            collective_id=0, has_side_effects=True, vmem_limit_bytes=36 * 2**20
        ),
        cost_estimate=pl.CostEstimate(flops=6 * 10**9, bytes_accessed=20 * 10**6, transcendentals=0),
        name="power_rounds",
    )(*(pltpu.with_memory_space_constraint(x, pltpu.HBM) for x in operands))


def update_kernel(
    shards,
    entries,
    corrected,
    left_ref,
    right_ref,
    total_ref,
    base_ref,
    momentum_ref,
    master_ref,
    table_ref,
    errors_out,
    factors_out,
    momentum_out,
    master_out,
    weights_out,
    table_out,
    errors_new,
    momentum_new,
    master_new,
    weights_new,
    esem,
    wsem,
    msem,
):
    shard = lax.axis_index("shard")
    rows = momentum_ref.shape[0]
    writes = [
        pltpu.make_async_copy(table_ref, table_out, msem.at[0]),
        pltpu.make_async_copy(right_ref, factors_out, msem.at[1]),
    ]
    for write in writes:
        write.start()
    right = right_ref[...]
    high, low = split(right)
    stacked = jnp.concatenate([high, high, low], axis=0)
    spread = jnp.sqrt(total_ref[0:1, 0:1] / entries + epsilon)
    clip = jnp.minimum(1.0, clip_level / spread)
    for i in range(shards):
        at = pl.ds(i * rows, rows)
        approx = jnp.dot(left_ref[at, :], stacked, preferred_element_type=f32)
        errors_new[at, :] = corrected[at, :] - approx
        write = pltpu.make_async_copy(errors_new.at[at], errors_out.at[at], esem.at[i])
        write.start()
        writes.append(write)
        clipped = clip * approx

        @pl.when(shard == i)
        def _():
            moved = momentum_decay * momentum_ref[...] + clipped
            stepped = master_ref[...] - learn_rate * moved
            momentum_new[...] = moved
            master_new[...] = stepped
            weights_new[at, :] = stepped.astype(bf16)

        @pl.when(shard != i)
        def _():
            weights_new[at, :] = (base_ref[i].astype(f32) - learn_rate * clipped).astype(bf16)

        write = pltpu.make_async_copy(weights_new.at[at], weights_out.at[at], wsem.at[i])
        write.start()
        writes.append(write)
    for write in (
        pltpu.make_async_copy(momentum_new, momentum_out, msem.at[2]),
        pltpu.make_async_copy(master_new, master_out, msem.at[3]),
    ):
        write.start()
        writes.append(write)
    for write in writes:
        write.wait()


def run_update(shards, entries, corrected, left, right, total, base, momentum, master, table):
    depth, width = corrected.shape
    hbm = pl.BlockSpec(memory_space=pltpu.HBM)
    vmem = pl.BlockSpec(memory_space=pltpu.VMEM)
    return pl.pallas_call(
        functools.partial(update_kernel, shards, entries),
        out_shape=(
            jax.ShapeDtypeStruct((depth, width), f32),
            jax.ShapeDtypeStruct(right.shape, f32),
            jax.ShapeDtypeStruct(momentum.shape, f32),
            jax.ShapeDtypeStruct(master.shape, f32),
            jax.ShapeDtypeStruct((depth, width), bf16),
            jax.ShapeDtypeStruct(table.shape, bf16),
        ),
        in_specs=[vmem] * 8,
        out_specs=(hbm,) * 6,
        scratch_shapes=[
            pltpu.VMEM((depth, width), f32),
            pltpu.VMEM(momentum.shape, f32),
            pltpu.VMEM(master.shape, f32),
            pltpu.VMEM((depth, width), bf16),
            pltpu.SemaphoreType.DMA((shards,)),
            pltpu.SemaphoreType.DMA((shards,)),
            pltpu.SemaphoreType.DMA((4,)),
        ],
        compiler_params=pltpu.CompilerParams(vmem_limit_bytes=30 * 2**20),
        name="apply_update",
    )(corrected, left, right, total, base, momentum, master, table)


def solution(mesh):
    shards, tensors, sections = (mesh.shape[a] for a in ("shard", "tensor", "section"))
    sizes = (shards, tensors, sections)

    def on_device(
        hidden_acts, out_grads, errors, factors, whiten, momentum, master, table, touched_ids, touched_grads
    ):
        power = run_power(
            sizes, table.shape[0], hidden_acts[0], out_grads[0], errors[0, 0], factors[0], whiten[0],
            momentum[0], master[0], table, touched_ids[None], touched_grads,
        )
        depth, width = errors.shape[2:]
        entries = sections * depth * width * tensors
        new_errors, new_factors, new_momentum, new_master, new_weights, new_table = run_update(
            shards, entries, *power
        )
        return (
            new_errors[None, None],
            new_factors[None],
            new_momentum[None],
            new_master[None],
            new_weights[None],
            new_table,
        )

    in_specs = (
        P("section", "shard", "tensor"),
        P("section", "shard", None),
        P("section", "shard", None, "tensor"),
        P("section", None, "tensor"),
        P("section", None, None, None),
        P("section", "shard", "tensor"),
        P("section", "shard", "tensor"),
        P(("shard", "section"), "tensor"),
        P(("shard", "section")),
        P(("shard", "section"), "tensor"),
    )
    out_specs = (
        P("section", "shard", None, "tensor"),
        P("section", None, "tensor"),
        P("section", "shard", "tensor"),
        P("section", "shard", "tensor"),
        P("section", None, "tensor"),
        P(("shard", "section"), "tensor"),
    )
    return jax.shard_map(on_device, mesh=mesh, in_specs=in_specs, out_specs=out_specs, check_vma=False)
```

```python
import functools

import jax
import jax.numpy as jnp
from jax import lax
from jax.experimental import pallas as pl
from jax.experimental.pallas import tpu as pltpu
from jax.sharding import PartitionSpec as P

ROUNDS = 2
LANES = 128
PIECE_ROWS = 32
CHUNKS = 5
TILE = 512
TABLE_ROWS = 1024

epsilon = 1e-06
momentum_decay = 0.9
learn_rate = 0.1
embed_rate = 0.25
clip_level = 0.03
highest = lax.Precision.HIGHEST
f32 = jnp.float32
bf16 = jnp.bfloat16
MESH = pl.DeviceIdType.MESH


def split(x):
    high = x.astype(bf16)
    low = (x - high.astype(f32)).astype(bf16)
    return high, low


def pieces(rank, width, count):
    rows = rank * (width // LANES) // count
    step = min(rows, rank)
    out = []
    for g in range(count):
        parts = []
        for at in range(0, rows, step):
            flat = g * rows + at
            parts.append((at, flat % rank, flat // rank * LANES, step))
        out.append(parts)
    return rows, out


def pack_rows(ids, touched, vocab, packed):
    owners, cap, _ = packed.shape
    count = touched.shape[0]
    owner = ids // vocab
    place = ids - owner * vocab
    owned = lax.broadcasted_iota(jnp.int32, (owners, count), 0) == owner
    before = lax.broadcasted_iota(jnp.int32, (count, count), 0) < lax.broadcasted_iota(
        jnp.int32, (count, count), 1
    )
    one = lambda mask: jnp.where(mask, 1.0, 0.0)
    ranks = jnp.dot(one(owned).astype(bf16), one(before).astype(bf16), preferred_element_type=f32)
    rank = jnp.sum(jnp.where(owned, ranks, 0.0), axis=0, keepdims=True)
    slot = owner * cap + rank.astype(jnp.int32)
    chosen = one(lax.broadcasted_iota(jnp.int32, (owners * cap, count), 0) == slot).astype(bf16)
    line = lax.broadcasted_iota(jnp.int32, (LANES, count), 0)
    coarse, fine = place // 128, place % 128
    notes = jnp.where(line == 0, coarse, jnp.where(line == 1, fine, jnp.where(line == 2, 1, 0)))
    sent = jnp.dot(chosen, touched, preferred_element_type=f32)
    sent_notes = jnp.dot(chosen, notes.astype(f32).T.astype(bf16), preferred_element_type=f32)
    width = touched.shape[1]
    for b in range(owners):
        packed[b, :, :width] = sent[b * cap : (b + 1) * cap].astype(bf16)
        packed[b, :, width:] = sent_notes[b * cap : (b + 1) * cap].astype(bf16)


def power_kernel(
    sizes,
    vocab,
    hidden_hbm,
    grads_hbm,
    errors_hbm,
    factors_hbm,
    whiten_hbm,
    momentum_hbm,
    master_hbm,
    table_hbm,
    ids_hbm,
    touched_hbm,
    corrected,
    left_ref,
    right_ref,
    total_ref,
    base_ref,
    momentum_ref,
    master_ref,
    table_ref,
    hidden,
    grads,
    errors,
    factors,
    whiten,
    ids,
    touched,
    high_ref,
    low_ref,
    lsend,
    lrecv,
    lgath,
    rsend0,
    rrecv0,
    rgath0,
    rsend1,
    rrecv1,
    rgath1,
    square,
    full,
    half,
    packed,
    found,
    lsem,
    rsem,
    qsem,
    tsem,
    bsem,
    msem,
    hsem,
    gsem,
):
    shards, tensors, sections = sizes
    rank, width = factors.shape
    depth = corrected.shape[0]
    tokens = hidden.shape[0]
    shard = lax.axis_index("shard")
    tensor = lax.axis_index("tensor")
    section = lax.axis_index("section")
    group = shards * tensors
    me = shard * tensors + tensor
    everyone = group * sections
    me_all = me * sections + section
    owners, cap, _ = packed.shape
    block = shard * sections + section

    def left_peer(k):
        index = lax.rem(me + k, group)
        return index, {"shard": index // tensors, "tensor": lax.rem(index, tensors)}

    def right_peer(k):
        index = lax.rem(shard + k, shards)
        return index, {"shard": index}

    def any_peer(k):
        index = lax.rem(me_all + k, everyone)
        pair = index // sections
        return index, {
            "shard": pair // tensors,
            "tensor": lax.rem(pair, tensors),
            "section": lax.rem(index, sections),
        }

    small = [
        (momentum_hbm, momentum_ref),
        (master_hbm, master_ref),
        (ids_hbm, ids),
        (touched_hbm, touched),
        (factors_hbm, factors),
        (whiten_hbm, whiten),
        (errors_hbm, errors),
        (table_hbm, table_ref),
    ]
    load = [pltpu.make_async_copy(src, dst, msem.at[i]) for i, (src, dst) in enumerate(small)]
    deep = tokens // CHUNKS
    acts = lambda k: pltpu.make_async_copy(
        hidden_hbm.at[pl.ds(k * deep, deep)], hidden.at[pl.ds(k * deep, deep)], hsem.at[k]
    )
    outs = lambda k: pltpu.make_async_copy(
        grads_hbm.at[pl.ds(k * deep, deep)], grads.at[pl.ds(k * deep, deep)], gsem.at[k]
    )
    for k in range(CHUNKS):
        outs(k).start()
        acts(k).start()
        if k == 0:
            for i in range(4):
                load[i].start()
    for i in range(4, 8):
        load[i].start()

    barrier = pltpu.get_barrier_semaphore()

    @pl.loop(1, everyone)
    def _(k):
        pl.semaphore_signal(barrier, inc=1, device_id=any_peer(k)[1], device_id_type=MESH)

    def deliver(k):
        index = lax.rem(block + k, owners)
        return pltpu.make_async_remote_copy(
            src_ref=packed.at[index],
            dst_ref=found.at[block],
            send_sem=tsem.at[0, k],
            recv_sem=tsem.at[1, k],
            device_id={"shard": index // sections, "section": lax.rem(index, sections)},
            device_id_type=MESH,
        )

    rows_own = base_ref.shape[1]
    piece = min(PIECE_ROWS, rows_own)
    per_block = rows_own // piece
    steps = shards - 1
    n_pieces = steps * per_block
    taken = [0]

    def carry(way, q, receiving=False):
        step, part = q // per_block, q % per_block
        sign = 1 if way == 0 else -1
        at = shard - sign if receiving else shard
        index = lax.rem(at - sign * step + 2 * shards, shards)
        rows = pl.ds(part * piece, piece)
        return pltpu.make_async_remote_copy(
            src_ref=base_ref.at[index, rows],
            dst_ref=base_ref.at[index, rows],
            send_sem=bsem.at[way, 0, q],
            recv_sem=bsem.at[way, 1, q],
            device_id={"shard": lax.rem(shard + sign + shards, shards)},
            device_id_type=MESH,
        )

    def sends(way, q):
        step = q // per_block
        if way == 0:
            return jnp.logical_and(shard >= step, shard < shards - 1)
        return jnp.logical_and(shard < shards - step, shard > 0)

    def arrives(way, q):
        step = q // per_block
        return shard >= step + 1 if way == 0 else shard < shards - 1 - step

    def arrive(q):
        for way in (0, 1):

            @pl.when(arrives(way, q))
            def _():
                carry(way, q, True).wait_recv()

    def pump(count):
        for q in range(taken[0], min(n_pieces, taken[0] + count)):
            if q >= per_block:
                arrive(q - per_block)
            for way in (0, 1):

                @pl.when(sends(way, q))
                def _():
                    carry(way, q).start()

            taken[0] = q + 1

    slots = [(n_pieces * share + 23) // 24 for share in PACE]
    slot = [0]

    def next_slot():
        pump(slots[slot[0]])
        slot[0] += 1

    tiles = depth // TILE
    for k in range(CHUNKS):
        outs(k).wait()
        acts(k).wait()
        at = slice(k * deep, (k + 1) * deep)
        for j in range(tiles):
            rows = slice(j * TILE, (j + 1) * TILE)
            part = lax.dot_general(
                grads[at, rows], hidden[at, :], (((0,), (0,)), ((), ())), preferred_element_type=f32
            )
            if k == 0:
                corrected[rows, :] = part
            elif k < CHUNKS - 1:
                corrected[rows, :] += part
            else:
                if j == 0:
                    load[6].wait()
                    load[4].wait()
                    load[5].wait()
                summed = (corrected[rows, :] + part).astype(bf16).astype(f32) + errors[rows, :]
                corrected[rows, :] = summed
                high, low = split(summed)
                high_ref[rows, :] = high
                low_ref[rows, :] = low
        if k == 0:
            load[0].wait()
            load[1].wait()
            own_base = master_ref[...] - (learn_rate * momentum_decay) * momentum_ref[...]
            base_ref[shard] = own_base.astype(bf16)
            pl.semaphore_wait(barrier, everyone - 1)
            next_slot()
        elif k == 1:
            load[2].wait()
            load[3].wait()
            pack_rows(ids[...], touched[...], vocab, packed)

            @pl.loop(1, owners)
            def _(k):
                deliver(k).start()

        if k < CHUNKS - 1:
            next_slot()

    def table_part(i):
        count = min(TABLE_ROWS, table_ref.shape[0])
        at = slice(i * count, (i + 1) * count)
        cols = table_ref.shape[1]
        rows = found[...].reshape(owners * cap, found.shape[2])
        notes = rows[:, cols:].astype(f32).T
        place = notes[0:1] * 128.0 + notes[1:2] - (1.0 - notes[2:3])
        index = place.astype(jnp.int32) - i * count
        places = lax.broadcasted_iota(jnp.int32, (count, index.shape[1]), 0)
        chosen = jnp.where(places == index, 1.0, 0.0).astype(bf16)
        table_grad = jnp.dot(chosen, rows[:, :cols], preferred_element_type=f32)
        table_ref[at, :] = (table_ref[at, :].astype(f32) - embed_rate * table_grad).astype(bf16)

    table_parts = max(1, table_ref.shape[0] // TABLE_ROWS)

    def delivered():
        @pl.loop(1, owners)
        def _(k):
            deliver(k).wait()

        found[block] = packed[block]
        load[7].wait()

    def start(count, copy):
        if count <= 16:
            for k in range(1, count):
                copy(k).start()
        else:

            @pl.loop(1, count)
            def _(k):
                copy(k).start()

    def finish(count, copy):
        @pl.loop(1, count)
        def _(k):
            copy(k).wait()

    def all_reduce(value, count, own, peer, send, recv, gath, sems, after, meanwhile, into):
        rows, cuts = pieces(value.shape[0], value.shape[1], count)
        wire = send.dtype
        value = value.astype(wire)
        for g in range(count):
            for at, row, col, step in cuts[g]:
                send[g, at : at + step, :] = value[row : row + step, col : col + LANES]

        def scatter(k):
            index, there = peer(k)
            return pltpu.make_async_remote_copy(
                src_ref=send.at[index],
                dst_ref=recv.at[k],
                send_sem=sems.at[0, k],
                recv_sem=sems.at[1, k],
                device_id=there,
                device_id_type=MESH,
            )

        start(count, scatter)
        next_slot()
        meanwhile[0]()
        finish(count, scatter)
        total = send[own].astype(f32)
        for k in range(1, count):
            total = total + recv[k].astype(f32)
        total = after(total)
        gath[own] = total.astype(gath.dtype)

        def gather(k):
            _, there = peer(k)
            return pltpu.make_async_remote_copy(
                src_ref=gath.at[own],
                dst_ref=gath.at[own],
                send_sem=sems.at[2, k],
                recv_sem=sems.at[3, k],
                device_id=there,
                device_id_type=MESH,
            )

        start(count, gather)
        meanwhile[1](total)
        next_slot()
        meanwhile[2]()
        finish(count, gather)
        next_slot()
        for g in range(count):
            for at, row, col, step in cuts[g]:
                into[row : row + step, col : col + LANES] = gath[g, at : at + step, :]
        return into[...]

    def times(x, dims, x_low, c_low):
        if x.dtype == bf16:
            return lax.dot_general(x, high_ref[...], (dims, ((), ())), preferred_element_type=f32)
        high, low = split(x)
        both = jnp.concatenate([high, low], axis=0)
        first = lax.dot_general(both, high_ref[...], (dims, ((), ())), preferred_element_type=f32)
        out = first[rank:]
        if c_low:
            out = out + lax.dot_general(high, low_ref[...], (dims, ((), ())), preferred_element_type=f32)
        return first[:rank] + out

    last = (((1,), (1,)), ((), ()))
    idle = lambda *_: None
    same = lambda x: x

    def share(k):
        _, there = any_peer(k)
        return pltpu.make_async_remote_copy(
            src_ref=square.at[0],
            dst_ref=square.at[k],
            send_sem=qsem.at[0, k],
            recv_sem=qsem.at[1, k],
            device_id=there,
            device_id_type=MESH,
        )

    table_at = [0]

    def some_table():
        if table_at[0] == 0:
            delivered()
        if table_at[0] < table_parts:
            table_part(table_at[0])
        table_at[0] += 1

    right = factors[...]
    for turn in range(ROUNDS):
        final = turn == ROUNDS - 1
        left_part = times(right, ((1,), (1,)), turn == 0, turn == 0)
        busy = some_table if turn > 0 else idle
        left = all_reduce(
            left_part, group, me, left_peer, lsend.at[turn], lrecv.at[turn], lgath.at[turn], lsem.at[turn],
            same, (busy, idle, busy), half if lgath.dtype == bf16 else full,
        )
        whitened = lax.dot_general(
            whiten[turn], left.astype(f32), (((0,), (0,)), ((), ())), precision=highest, preferred_element_type=f32
        )
        scale = lax.rsqrt(jnp.sum(whitened * whitened) / rank + epsilon)
        right_part = times(whitened, ((1,), (0,)), True, final)
        rsend, rrecv, rgath = (rsend1, rrecv1, rgath1) if final else (rsend0, rrecv0, rgath0)
        into = half if rgath.dtype == bf16 else full
        if not final:
            right = all_reduce(
                right_part, shards, shard, right_peer, rsend, rrecv, rgath, rsem.at[turn],
                lambda x: x * (scale * (1.0 / shards)), (some_table, idle, some_table), into,
            )
            continue
        left_unit = whitened * scale
        kept = []

        def prepare():
            left_high = left_unit.astype(bf16).astype(f32)
            stacked = jnp.concatenate([left_high, left_unit - left_high, left_high], axis=0)
            left_ref[...] = stacked.T.astype(bf16)
            kept.append(lax.dot_general(left_unit, left_unit, last, precision=highest, preferred_element_type=f32))

        def announce(gram_right, weight):
            amount = jnp.sum(kept[0] * gram_right) * weight
            square[0] = jnp.full(square.shape[1:], amount, f32)
            start(everyone, share)

        def own_squares(total):
            if total.shape[0] % rank:
                return
            gram = None
            for at in range(0, total.shape[0], rank):
                cols = total[at : at + rank]
                term = lax.dot_general(cols, cols, last, precision=highest, preferred_element_type=f32)
                gram = term if gram is None else gram + term
            announce(gram, 1.0)

        right = all_reduce(
            right_part, shards, shard, right_peer, rsend, rrecv, rgath, rsem.at[turn],
            lambda x: x * (scale * (1.0 / shards)), (prepare, own_squares, idle), into,
        )
        if rgath.shape[1] % rank:
            gram = lax.dot_general(right, right, last, precision=highest, preferred_element_type=f32)
            announce(gram, 1.0 / shards)

    right_ref[...] = right
    right_high, right_low = split(right)
    stacked_right = jnp.concatenate([right_high, right_high, right_low], axis=0)
    corrected[...] = corrected[...] - jnp.dot(left_ref[...], stacked_right, preferred_element_type=f32)
    while table_at[0] < table_parts:
        some_table()
    pump(n_pieces)
    for q in range(max(0, n_pieces - per_block), n_pieces):
        arrive(q)
    finish(everyone, share)
    total_ref[...] = jnp.broadcast_to(jnp.sum(square[...], axis=0), total_ref.shape)
    for q in range(n_pieces):
        for way in (0, 1):

            @pl.when(sends(way, q))
            def _():
                carry(way, q).wait_send()


PACE = (3, 0, 0, 0, 0, 2, 3, 0, 3, 2, 0, 3, 3, 0, 3, 2, 0)


def run_power(sizes, vocab, hidden, grads, errors, factors, whiten, momentum, master, table, ids, touched):
    shards, tensors, sections = sizes
    rank, width = factors.shape
    tokens, depth = grads.shape
    rows_own = momentum.shape[0]
    owners = shards * sections
    cap = 2 * touched.shape[0] // owners
    packed = (owners, cap, touched.shape[1] + LANES)
    group = shards * tensors
    everyone = group * sections
    left_rows = rank * (depth // LANES) // group
    right_rows = rank * (width // LANES) // shards
    operands = (hidden, grads, errors, factors, whiten, momentum, master, table, ids, touched)
    narrow = lambda rows: bf16 if rows % 16 == 0 else f32
    per_block = rows_own // min(PIECE_ROWS, rows_own)
    hbm = pl.BlockSpec(memory_space=pltpu.HBM)
    vmem = pl.BlockSpec(memory_space=pltpu.VMEM)
    return pl.pallas_call(
        functools.partial(power_kernel, sizes, vocab),
        out_shape=(
            jax.ShapeDtypeStruct((depth, width), f32),
            jax.ShapeDtypeStruct((depth, 3 * rank), bf16),
            jax.ShapeDtypeStruct((rank, width), f32),
            jax.ShapeDtypeStruct((8, LANES), f32),
            jax.ShapeDtypeStruct((shards, rows_own, width), bf16),
            jax.ShapeDtypeStruct(momentum.shape, f32),
            jax.ShapeDtypeStruct(master.shape, f32),
            jax.ShapeDtypeStruct(table.shape, bf16),
        ),
        in_specs=[hbm] * 10,
        out_specs=(vmem,) * 8,
        scratch_shapes=[
            pltpu.VMEM(hidden.shape, bf16),
            pltpu.VMEM(grads.shape, bf16),
            pltpu.VMEM(errors.shape, f32),
            pltpu.VMEM(factors.shape, f32),
            pltpu.VMEM(whiten.shape, f32),
            pltpu.VMEM(ids.shape, jnp.int32),
            pltpu.VMEM(touched.shape, bf16),
            pltpu.VMEM((depth, width), bf16),
            pltpu.VMEM((depth, width), bf16),
            pltpu.VMEM((ROUNDS, group, left_rows, LANES), narrow(left_rows)),
            pltpu.VMEM((ROUNDS, group, left_rows, LANES), narrow(left_rows)),
            pltpu.VMEM((ROUNDS, group, left_rows, LANES), narrow(left_rows)),
            pltpu.VMEM((shards, right_rows, LANES), narrow(right_rows)),
            pltpu.VMEM((shards, right_rows, LANES), narrow(right_rows)),
            pltpu.VMEM((shards, right_rows, LANES), narrow(right_rows)),
            pltpu.VMEM((shards, right_rows, LANES), f32),
            pltpu.VMEM((shards, right_rows, LANES), f32),
            pltpu.VMEM((shards, right_rows, LANES), f32),
            pltpu.VMEM((everyone, 1, LANES), f32),
            pltpu.VMEM((rank, max(depth, width)), f32),
            pltpu.VMEM((rank, max(depth, width)), bf16),
            pltpu.VMEM(packed, bf16),
            pltpu.VMEM(packed, bf16),
            pltpu.SemaphoreType.DMA((ROUNDS, 4, group)),
            pltpu.SemaphoreType.DMA((ROUNDS, 4, shards)),
            pltpu.SemaphoreType.DMA((2, everyone)),
            pltpu.SemaphoreType.DMA((2, owners)),
            pltpu.SemaphoreType.DMA((2, 2, (shards - 1) * per_block)),
            pltpu.SemaphoreType.DMA((8,)),
            pltpu.SemaphoreType.DMA((CHUNKS,)),
            pltpu.SemaphoreType.DMA((CHUNKS,)),
        ],
        compiler_params=pltpu.CompilerParams(
            collective_id=0, has_side_effects=True, vmem_limit_bytes=36 * 2**20
        ),
        cost_estimate=pl.CostEstimate(flops=6 * 10**9, bytes_accessed=20 * 10**6, transcendentals=0),
        name="power_rounds",
    )(*(pltpu.with_memory_space_constraint(x, pltpu.HBM) for x in operands))


def update_kernel(
    shards,
    entries,
    corrected,
    left_ref,
    right_ref,
    total_ref,
    base_ref,
    momentum_ref,
    master_ref,
    table_ref,
    errors_out,
    factors_out,
    momentum_out,
    master_out,
    weights_out,
    table_out,
    momentum_new,
    master_new,
    weights_new,
    wsem,
    msem,
):
    shard = lax.axis_index("shard")
    rows = momentum_ref.shape[0]
    writes = [
        pltpu.make_async_copy(table_ref, table_out, msem.at[0]),
        pltpu.make_async_copy(right_ref, factors_out, msem.at[1]),
        pltpu.make_async_copy(corrected, errors_out, msem.at[4]),
    ]
    for write in writes:
        write.start()
    right = right_ref[...]
    high, low = split(right)
    stacked = jnp.concatenate([high, high, low], axis=0)
    spread = jnp.sqrt(total_ref[0:1, 0:1] / entries + epsilon)
    clip = jnp.minimum(1.0, clip_level / spread)
    for i in range(shards):
        at = pl.ds(i * rows, rows)
        approx = jnp.dot(left_ref[at, :], stacked, preferred_element_type=f32)
        clipped = clip * approx

        @pl.when(shard == i)
        def _():
            moved = momentum_decay * momentum_ref[...] + clipped
            stepped = master_ref[...] - learn_rate * moved
            momentum_new[...] = moved
            master_new[...] = stepped
            weights_new[at, :] = stepped.astype(bf16)

        @pl.when(shard != i)
        def _():
            weights_new[at, :] = (base_ref[i].astype(f32) - learn_rate * clipped).astype(bf16)

        write = pltpu.make_async_copy(weights_new.at[at], weights_out.at[at], wsem.at[i])
        write.start()
        writes.append(write)
    for write in (
        pltpu.make_async_copy(momentum_new, momentum_out, msem.at[2]),
        pltpu.make_async_copy(master_new, master_out, msem.at[3]),
    ):
        write.start()
        writes.append(write)
    for write in writes:
        write.wait()


def run_update(shards, entries, corrected, left, right, total, base, momentum, master, table):
    depth, width = corrected.shape
    hbm = pl.BlockSpec(memory_space=pltpu.HBM)
    vmem = pl.BlockSpec(memory_space=pltpu.VMEM)
    return pl.pallas_call(
        functools.partial(update_kernel, shards, entries),
        out_shape=(
            jax.ShapeDtypeStruct((depth, width), f32),
            jax.ShapeDtypeStruct(right.shape, f32),
            jax.ShapeDtypeStruct(momentum.shape, f32),
            jax.ShapeDtypeStruct(master.shape, f32),
            jax.ShapeDtypeStruct((depth, width), bf16),
            jax.ShapeDtypeStruct(table.shape, bf16),
        ),
        in_specs=[vmem] * 8,
        out_specs=(hbm,) * 6,
        scratch_shapes=[
            pltpu.VMEM(momentum.shape, f32),
            pltpu.VMEM(master.shape, f32),
            pltpu.VMEM((depth, width), bf16),
            pltpu.SemaphoreType.DMA((shards,)),
            pltpu.SemaphoreType.DMA((5,)),
        ],
        compiler_params=pltpu.CompilerParams(vmem_limit_bytes=30 * 2**20),
        name="apply_update",
    )(corrected, left, right, total, base, momentum, master, table)


def solution(mesh):
    shards, tensors, sections = (mesh.shape[a] for a in ("shard", "tensor", "section"))
    sizes = (shards, tensors, sections)

    def on_device(
        hidden_acts, out_grads, errors, factors, whiten, momentum, master, table, touched_ids, touched_grads
    ):
        power = run_power(
            sizes, table.shape[0], hidden_acts[0], out_grads[0], errors[0, 0], factors[0], whiten[0],
            momentum[0], master[0], table, touched_ids[None], touched_grads,
        )
        depth, width = errors.shape[2:]
        entries = sections * depth * width * tensors
        new_errors, new_factors, new_momentum, new_master, new_weights, new_table = run_update(
            shards, entries, *power
        )
        return (
            new_errors[None, None],
            new_factors[None],
            new_momentum[None],
            new_master[None],
            new_weights[None],
            new_table,
        )

    in_specs = (
        P("section", "shard", "tensor"),
        P("section", "shard", None),
        P("section", "shard", None, "tensor"),
        P("section", None, "tensor"),
        P("section", None, None, None),
        P("section", "shard", "tensor"),
        P("section", "shard", "tensor"),
        P(("shard", "section"), "tensor"),
        P(("shard", "section")),
        P(("shard", "section"), "tensor"),
    )
    out_specs = (
        P("section", "shard", None, "tensor"),
        P("section", None, "tensor"),
        P("section", "shard", "tensor"),
        P("section", "shard", "tensor"),
        P("section", None, "tensor"),
        P(("shard", "section"), "tensor"),
    )
    return jax.shard_map(on_device, mesh=mesh, in_specs=in_specs, out_specs=out_specs, check_vma=False)
```

```python
import functools

import jax
import jax.numpy as jnp
from jax import lax
from jax.experimental import pallas as pl
from jax.experimental.pallas import tpu as pltpu
from jax.sharding import PartitionSpec as P

ROUNDS = 2
LANES = 128
PIECE_ROWS = 32
CHUNKS = 5
TILE = 512
TABLE_ROWS = 1024

epsilon = 1e-06
momentum_decay = 0.9
learn_rate = 0.1
embed_rate = 0.25
clip_level = 0.03
highest = lax.Precision.HIGHEST
f32 = jnp.float32
bf16 = jnp.bfloat16
MESH = pl.DeviceIdType.MESH


def split(x):
    high = x.astype(bf16)
    low = (x - high.astype(f32)).astype(bf16)
    return high, low


def pieces(rank, width, count):
    rows = rank * (width // LANES) // count
    step = min(rows, rank)
    out = []
    for g in range(count):
        parts = []
        for at in range(0, rows, step):
            flat = g * rows + at
            parts.append((at, flat % rank, flat // rank * LANES, step))
        out.append(parts)
    return rows, out


def pack_rows(ids, touched, vocab, packed, places):
    owners, cap, _ = packed.shape
    count = touched.shape[0]
    owner = ids // vocab
    place = ids - owner * vocab
    owned = lax.broadcasted_iota(jnp.int32, (owners, count), 0) == owner
    before = lax.broadcasted_iota(jnp.int32, (count, count), 0) < lax.broadcasted_iota(
        jnp.int32, (count, count), 1
    )
    one = lambda mask: jnp.where(mask, 1.0, 0.0)
    ranks = jnp.dot(one(owned).astype(bf16), one(before).astype(bf16), preferred_element_type=f32)
    rank = jnp.sum(jnp.where(owned, ranks, 0.0), axis=0, keepdims=True)
    slot = owner * cap + rank.astype(jnp.int32)
    chosen = one(lax.broadcasted_iota(jnp.int32, (owners * cap, count), 0) == slot).astype(bf16)
    line = lax.broadcasted_iota(jnp.int32, (places.shape[1], count), 0)
    coarse, fine = place // 128, place % 128
    notes = jnp.where(line == 0, coarse, jnp.where(line == 1, fine, jnp.where(line == 2, 1, 0)))
    sent = jnp.dot(chosen, touched, preferred_element_type=f32)
    sent_notes = lax.dot_general(
        notes.astype(f32).astype(bf16), chosen, (((1,), (1,)), ((), ())), preferred_element_type=f32
    )
    places[...] = jnp.zeros(places.shape, bf16)
    for b in range(owners):
        packed[b] = sent[b * cap : (b + 1) * cap].astype(bf16)
        places[b, :, :cap] = sent_notes[:, b * cap : (b + 1) * cap].astype(bf16)


def power_kernel(
    sizes,
    vocab,
    hidden_hbm,
    grads_hbm,
    errors_hbm,
    factors_hbm,
    whiten_hbm,
    momentum_hbm,
    master_hbm,
    table_hbm,
    ids_hbm,
    touched_hbm,
    corrected,
    left_ref,
    right_ref,
    total_ref,
    base_ref,
    momentum_ref,
    master_ref,
    table_ref,
    hidden,
    grads,
    errors,
    factors,
    whiten,
    ids,
    touched,
    high_ref,
    low_ref,
    lsend,
    lrecv,
    lgath,
    rsend0,
    rrecv0,
    rgath0,
    rsend1,
    rrecv1,
    rgath1,
    square,
    full,
    half,
    packed,
    found,
    places,
    found_places,
    lsem,
    rsem,
    qsem,
    tsem,
    bsem,
    msem,
    hsem,
    gsem,
):
    shards, tensors, sections = sizes
    rank, width = factors.shape
    depth = corrected.shape[0]
    tokens = hidden.shape[0]
    shard = lax.axis_index("shard")
    tensor = lax.axis_index("tensor")
    section = lax.axis_index("section")
    group = shards * tensors
    me = shard * tensors + tensor
    everyone = group * sections
    me_all = me * sections + section
    owners, cap, _ = packed.shape
    block = shard * sections + section

    def left_peer(k):
        index = lax.rem(me + k, group)
        return index, {"shard": index // tensors, "tensor": lax.rem(index, tensors)}

    def right_peer(k):
        index = lax.rem(shard + k, shards)
        return index, {"shard": index}

    def any_peer(k):
        index = lax.rem(me_all + k, everyone)
        pair = index // sections
        return index, {
            "shard": pair // tensors,
            "tensor": lax.rem(pair, tensors),
            "section": lax.rem(index, sections),
        }

    small = [
        (momentum_hbm, momentum_ref),
        (master_hbm, master_ref),
        (ids_hbm, ids),
        (touched_hbm, touched),
        (factors_hbm, factors),
        (whiten_hbm, whiten),
        (errors_hbm, errors),
        (table_hbm, table_ref),
    ]
    load = [pltpu.make_async_copy(src, dst, msem.at[i]) for i, (src, dst) in enumerate(small)]
    deep = tokens // CHUNKS
    acts = lambda k: pltpu.make_async_copy(
        hidden_hbm.at[pl.ds(k * deep, deep)], hidden.at[pl.ds(k * deep, deep)], hsem.at[k]
    )
    outs = lambda k: pltpu.make_async_copy(
        grads_hbm.at[pl.ds(k * deep, deep)], grads.at[pl.ds(k * deep, deep)], gsem.at[k]
    )
    for k in range(CHUNKS):
        outs(k).start()
        acts(k).start()
        if k == 0:
            for i in range(4):
                load[i].start()
    for i in range(4, 8):
        load[i].start()

    barrier = pltpu.get_barrier_semaphore()

    @pl.loop(1, everyone)
    def _(k):
        pl.semaphore_signal(barrier, inc=1, device_id=any_peer(k)[1], device_id_type=MESH)

    def deliver(k, what):
        index = lax.rem(block + k, owners)
        source, target = ((packed, found), (places, found_places))[what]
        return pltpu.make_async_remote_copy(
            src_ref=source.at[index],
            dst_ref=target.at[block],
            send_sem=tsem.at[what, 0, k],
            recv_sem=tsem.at[what, 1, k],
            device_id={"shard": index // sections, "section": lax.rem(index, sections)},
            device_id_type=MESH,
        )

    rows_own = base_ref.shape[1]
    piece = min(PIECE_ROWS, rows_own)
    per_block = rows_own // piece
    steps = shards - 1
    n_pieces = steps * per_block
    taken = [0]

    def carry(way, q, receiving=False):
        step, part = q // per_block, q % per_block
        sign = 1 if way == 0 else -1
        at = shard - sign if receiving else shard
        index = lax.rem(at - sign * step + 2 * shards, shards)
        rows = pl.ds(part * piece, piece)
        return pltpu.make_async_remote_copy(
            src_ref=base_ref.at[index, rows],
            dst_ref=base_ref.at[index, rows],
            send_sem=bsem.at[way, 0, q],
            recv_sem=bsem.at[way, 1, q],
            device_id={"shard": lax.rem(shard + sign + shards, shards)},
            device_id_type=MESH,
        )

    def sends(way, q):
        step = q // per_block
        if way == 0:
            return jnp.logical_and(shard >= step, shard < shards - 1)
        return jnp.logical_and(shard < shards - step, shard > 0)

    def arrives(way, q):
        step = q // per_block
        return shard >= step + 1 if way == 0 else shard < shards - 1 - step

    def arrive(q):
        for way in (0, 1):

            @pl.when(arrives(way, q))
            def _():
                carry(way, q, True).wait_recv()

    def pump(count):
        for q in range(taken[0], min(n_pieces, taken[0] + count)):
            if q >= per_block:
                arrive(q - per_block)
            for way in (0, 1):

                @pl.when(sends(way, q))
                def _():
                    carry(way, q).start()

            taken[0] = q + 1

    slots = [(n_pieces * share + 23) // 24 for share in PACE]
    slot = [0]

    def next_slot():
        pump(slots[slot[0]])
        slot[0] += 1

    tiles = depth // TILE
    for k in range(CHUNKS):
        outs(k).wait()
        acts(k).wait()
        at = slice(k * deep, (k + 1) * deep)
        for j in range(tiles):
            rows = slice(j * TILE, (j + 1) * TILE)
            part = lax.dot_general(
                grads[at, rows], hidden[at, :], (((0,), (0,)), ((), ())), preferred_element_type=f32
            )
            if k == 0:
                corrected[rows, :] = part
            elif k < CHUNKS - 1:
                corrected[rows, :] += part
            else:
                if j == 0:
                    load[6].wait()
                    load[4].wait()
                    load[5].wait()
                summed = (corrected[rows, :] + part).astype(bf16).astype(f32) + errors[rows, :]
                corrected[rows, :] = summed
                high, low = split(summed)
                high_ref[rows, :] = high
                low_ref[rows, :] = low
        if k == 0:
            load[0].wait()
            load[1].wait()
            own_base = master_ref[...] - (learn_rate * momentum_decay) * momentum_ref[...]
            base_ref[shard] = own_base.astype(bf16)
            pl.semaphore_wait(barrier, everyone - 1)
            next_slot()
        elif k == 1:
            load[2].wait()
            load[3].wait()
            pack_rows(ids[...], touched[...], vocab, packed, places)

            @pl.loop(1, owners)
            def _(k):
                deliver(k, 0).start()
                deliver(k, 1).start()

        if k < CHUNKS - 1:
            next_slot()

    def table_part(i):
        count = min(TABLE_ROWS, table_ref.shape[0])
        at = slice(i * count, (i + 1) * count)
        cols = table_ref.shape[1]
        rows = found[...].reshape(owners * cap, found.shape[2])
        notes = jnp.concatenate([found_places[b][:, :cap] for b in range(owners)], axis=1).astype(f32)
        place = notes[0:1] * 128.0 + notes[1:2] - (1.0 - notes[2:3])
        index = place.astype(jnp.int32) - i * count
        places = lax.broadcasted_iota(jnp.int32, (count, index.shape[1]), 0)
        chosen = jnp.where(places == index, 1.0, 0.0).astype(bf16)
        table_grad = jnp.dot(chosen, rows, preferred_element_type=f32)
        table_ref[at, :] = (table_ref[at, :].astype(f32) - embed_rate * table_grad).astype(bf16)

    table_parts = max(1, table_ref.shape[0] // TABLE_ROWS)

    def delivered():
        @pl.loop(1, owners)
        def _(k):
            deliver(k, 0).wait()
            deliver(k, 1).wait()

        found[block] = packed[block]
        found_places[block] = places[block]
        load[7].wait()

    def start(count, copy):
        if count <= 16:
            for k in range(1, count):
                copy(k).start()
        else:

            @pl.loop(1, count)
            def _(k):
                copy(k).start()

    def finish(count, copy):
        @pl.loop(1, count)
        def _(k):
            copy(k).wait()

    def all_reduce(value, count, own, peer, send, recv, gath, sems, after, meanwhile, into):
        rows, cuts = pieces(value.shape[0], value.shape[1], count)
        wire = send.dtype
        value = value.astype(wire)
        for g in range(count):
            for at, row, col, step in cuts[g]:
                send[g, at : at + step, :] = value[row : row + step, col : col + LANES]

        def scatter(k):
            index, there = peer(k)
            return pltpu.make_async_remote_copy(
                src_ref=send.at[index],
                dst_ref=recv.at[k],
                send_sem=sems.at[0, k],
                recv_sem=sems.at[1, k],
                device_id=there,
                device_id_type=MESH,
            )

        start(count, scatter)
        next_slot()
        meanwhile[0]()
        finish(count, scatter)
        total = send[own].astype(f32)
        for k in range(1, count):
            total = total + recv[k].astype(f32)
        total = after(total)
        gath[own] = total.astype(gath.dtype)

        def gather(k):
            _, there = peer(k)
            return pltpu.make_async_remote_copy(
                src_ref=gath.at[own],
                dst_ref=gath.at[own],
                send_sem=sems.at[2, k],
                recv_sem=sems.at[3, k],
                device_id=there,
                device_id_type=MESH,
            )

        start(count, gather)
        meanwhile[1](total)
        next_slot()
        meanwhile[2]()
        finish(count, gather)
        next_slot()
        for g in range(count):
            for at, row, col, step in cuts[g]:
                into[row : row + step, col : col + LANES] = gath[g, at : at + step, :]
        return into[...]

    def times(x, dims, x_low, c_low):
        if x.dtype == bf16:
            return lax.dot_general(x, high_ref[...], (dims, ((), ())), preferred_element_type=f32)
        high, low = split(x)
        both = jnp.concatenate([high, low], axis=0)
        first = lax.dot_general(both, high_ref[...], (dims, ((), ())), preferred_element_type=f32)
        out = first[rank:]
        if c_low:
            out = out + lax.dot_general(high, low_ref[...], (dims, ((), ())), preferred_element_type=f32)
        return first[:rank] + out

    last = (((1,), (1,)), ((), ()))
    idle = lambda *_: None
    same = lambda x: x

    def share(k):
        _, there = any_peer(k)
        return pltpu.make_async_remote_copy(
            src_ref=square.at[0],
            dst_ref=square.at[k],
            send_sem=qsem.at[0, k],
            recv_sem=qsem.at[1, k],
            device_id=there,
            device_id_type=MESH,
        )

    table_at = [0]

    def some_table():
        if table_at[0] == 0:
            delivered()
        if table_at[0] < table_parts:
            table_part(table_at[0])
        table_at[0] += 1

    right = factors[...]
    for turn in range(ROUNDS):
        final = turn == ROUNDS - 1
        left_part = times(right, ((1,), (1,)), turn == 0, turn == 0)
        busy = some_table if turn > 0 else idle
        left = all_reduce(
            left_part, group, me, left_peer, lsend.at[turn], lrecv.at[turn], lgath.at[turn], lsem.at[turn],
            same, (busy, idle, busy), half if lgath.dtype == bf16 else full,
        )
        whitened = lax.dot_general(
            whiten[turn], left.astype(f32), (((0,), (0,)), ((), ())), precision=highest, preferred_element_type=f32
        )
        scale = lax.rsqrt(jnp.sum(whitened * whitened) / rank + epsilon)
        right_part = times(whitened, ((1,), (0,)), True, final)
        rsend, rrecv, rgath = (rsend1, rrecv1, rgath1) if final else (rsend0, rrecv0, rgath0)
        into = half if rgath.dtype == bf16 else full
        if not final:
            right = all_reduce(
                right_part, shards, shard, right_peer, rsend, rrecv, rgath, rsem.at[turn],
                lambda x: x * (scale * (1.0 / shards)), (some_table, idle, some_table), into,
            )
            continue
        left_unit = whitened * scale
        kept = []

        def prepare():
            left_high = left_unit.astype(bf16).astype(f32)
            stacked = jnp.concatenate([left_high, left_unit - left_high, left_high], axis=0)
            left_ref[...] = stacked.T.astype(bf16)
            kept.append(lax.dot_general(left_unit, left_unit, last, precision=highest, preferred_element_type=f32))

        def announce(gram_right, weight):
            amount = jnp.sum(kept[0] * gram_right) * weight
            square[0] = jnp.full(square.shape[1:], amount, f32)
            start(everyone, share)

        def own_squares(total):
            if total.shape[0] % rank:
                return
            gram = None
            for at in range(0, total.shape[0], rank):
                cols = total[at : at + rank]
                term = lax.dot_general(cols, cols, last, precision=highest, preferred_element_type=f32)
                gram = term if gram is None else gram + term
            announce(gram, 1.0)

        right = all_reduce(
            right_part, shards, shard, right_peer, rsend, rrecv, rgath, rsem.at[turn],
            lambda x: x * (scale * (1.0 / shards)), (prepare, own_squares, idle), into,
        )
        if rgath.shape[1] % rank:
            gram = lax.dot_general(right, right, last, precision=highest, preferred_element_type=f32)
            announce(gram, 1.0 / shards)

    right_ref[...] = right
    right_high, right_low = split(right)
    stacked_right = jnp.concatenate([right_high, right_high, right_low], axis=0)
    corrected[...] = corrected[...] - jnp.dot(left_ref[...], stacked_right, preferred_element_type=f32)
    while table_at[0] < table_parts:
        some_table()
    pump(n_pieces)
    for q in range(max(0, n_pieces - per_block), n_pieces):
        arrive(q)
    finish(everyone, share)
    total_ref[...] = jnp.broadcast_to(jnp.sum(square[...], axis=0), total_ref.shape)
    for q in range(n_pieces):
        for way in (0, 1):

            @pl.when(sends(way, q))
            def _():
                carry(way, q).wait_send()


PACE = (3, 0, 0, 0, 0, 2, 3, 0, 3, 3, 0, 3, 3, 0, 3, 1, 0)


def run_power(sizes, vocab, hidden, grads, errors, factors, whiten, momentum, master, table, ids, touched):
    shards, tensors, sections = sizes
    rank, width = factors.shape
    tokens, depth = grads.shape
    rows_own = momentum.shape[0]
    owners = shards * sections
    cap = 2 * touched.shape[0] // owners
    packed = (owners, cap, touched.shape[1])
    places = (owners, 16, LANES)
    group = shards * tensors
    everyone = group * sections
    left_rows = rank * (depth // LANES) // group
    right_rows = rank * (width // LANES) // shards
    operands = (hidden, grads, errors, factors, whiten, momentum, master, table, ids, touched)
    narrow = lambda rows: bf16 if rows % 16 == 0 else f32
    per_block = rows_own // min(PIECE_ROWS, rows_own)
    hbm = pl.BlockSpec(memory_space=pltpu.HBM)
    vmem = pl.BlockSpec(memory_space=pltpu.VMEM)
    return pl.pallas_call(
        functools.partial(power_kernel, sizes, vocab),
        out_shape=(
            jax.ShapeDtypeStruct((depth, width), f32),
            jax.ShapeDtypeStruct((depth, 3 * rank), bf16),
            jax.ShapeDtypeStruct((rank, width), f32),
            jax.ShapeDtypeStruct((8, LANES), f32),
            jax.ShapeDtypeStruct((shards, rows_own, width), bf16),
            jax.ShapeDtypeStruct(momentum.shape, f32),
            jax.ShapeDtypeStruct(master.shape, f32),
            jax.ShapeDtypeStruct(table.shape, bf16),
        ),
        in_specs=[hbm] * 10,
        out_specs=(vmem,) * 8,
        scratch_shapes=[
            pltpu.VMEM(hidden.shape, bf16),
            pltpu.VMEM(grads.shape, bf16),
            pltpu.VMEM(errors.shape, f32),
            pltpu.VMEM(factors.shape, f32),
            pltpu.VMEM(whiten.shape, f32),
            pltpu.VMEM(ids.shape, jnp.int32),
            pltpu.VMEM(touched.shape, bf16),
            pltpu.VMEM((depth, width), bf16),
            pltpu.VMEM((depth, width), bf16),
            pltpu.VMEM((ROUNDS, group, left_rows, LANES), narrow(left_rows)),
            pltpu.VMEM((ROUNDS, group, left_rows, LANES), narrow(left_rows)),
            pltpu.VMEM((ROUNDS, group, left_rows, LANES), narrow(left_rows)),
            pltpu.VMEM((shards, right_rows, LANES), narrow(right_rows)),
            pltpu.VMEM((shards, right_rows, LANES), narrow(right_rows)),
            pltpu.VMEM((shards, right_rows, LANES), narrow(right_rows)),
            pltpu.VMEM((shards, right_rows, LANES), f32),
            pltpu.VMEM((shards, right_rows, LANES), f32),
            pltpu.VMEM((shards, right_rows, LANES), f32),
            pltpu.VMEM((everyone, 1, LANES), f32),
            pltpu.VMEM((rank, max(depth, width)), f32),
            pltpu.VMEM((rank, max(depth, width)), bf16),
            pltpu.VMEM(packed, bf16),
            pltpu.VMEM(packed, bf16),
            pltpu.VMEM(places, bf16),
            pltpu.VMEM(places, bf16),
            pltpu.SemaphoreType.DMA((ROUNDS, 4, group)),
            pltpu.SemaphoreType.DMA((ROUNDS, 4, shards)),
            pltpu.SemaphoreType.DMA((2, everyone)),
            pltpu.SemaphoreType.DMA((2, 2, owners)),
            pltpu.SemaphoreType.DMA((2, 2, (shards - 1) * per_block)),
            pltpu.SemaphoreType.DMA((8,)),
            pltpu.SemaphoreType.DMA((CHUNKS,)),
            pltpu.SemaphoreType.DMA((CHUNKS,)),
        ],
        compiler_params=pltpu.CompilerParams(
            collective_id=0, has_side_effects=True, vmem_limit_bytes=36 * 2**20
        ),
        cost_estimate=pl.CostEstimate(flops=6 * 10**9, bytes_accessed=20 * 10**6, transcendentals=0),
        name="power_rounds",
    )(*(pltpu.with_memory_space_constraint(x, pltpu.HBM) for x in operands))


def update_kernel(
    shards,
    entries,
    corrected,
    left_ref,
    right_ref,
    total_ref,
    base_ref,
    momentum_ref,
    master_ref,
    table_ref,
    errors_out,
    factors_out,
    momentum_out,
    master_out,
    weights_out,
    table_out,
    momentum_new,
    master_new,
    weights_new,
    wsem,
    msem,
):
    shard = lax.axis_index("shard")
    rows = momentum_ref.shape[0]
    writes = [
        pltpu.make_async_copy(table_ref, table_out, msem.at[0]),
        pltpu.make_async_copy(right_ref, factors_out, msem.at[1]),
        pltpu.make_async_copy(corrected, errors_out, msem.at[4]),
    ]
    for write in writes:
        write.start()
    right = right_ref[...]
    high, low = split(right)
    stacked = jnp.concatenate([high, high, low], axis=0)
    spread = jnp.sqrt(total_ref[0:1, 0:1] / entries + epsilon)
    clip = jnp.minimum(1.0, clip_level / spread)
    for i in range(shards):
        at = pl.ds(i * rows, rows)
        approx = jnp.dot(left_ref[at, :], stacked, preferred_element_type=f32)
        clipped = clip * approx

        @pl.when(shard == i)
        def _():
            moved = momentum_decay * momentum_ref[...] + clipped
            stepped = master_ref[...] - learn_rate * moved
            momentum_new[...] = moved
            master_new[...] = stepped
            weights_new[at, :] = stepped.astype(bf16)

        @pl.when(shard != i)
        def _():
            weights_new[at, :] = (base_ref[i].astype(f32) - learn_rate * clipped).astype(bf16)

        write = pltpu.make_async_copy(weights_new.at[at], weights_out.at[at], wsem.at[i])
        write.start()
        writes.append(write)
    for write in (
        pltpu.make_async_copy(momentum_new, momentum_out, msem.at[2]),
        pltpu.make_async_copy(master_new, master_out, msem.at[3]),
    ):
        write.start()
        writes.append(write)
    for write in writes:
        write.wait()


def run_update(shards, entries, corrected, left, right, total, base, momentum, master, table):
    depth, width = corrected.shape
    hbm = pl.BlockSpec(memory_space=pltpu.HBM)
    vmem = pl.BlockSpec(memory_space=pltpu.VMEM)
    return pl.pallas_call(
        functools.partial(update_kernel, shards, entries),
        out_shape=(
            jax.ShapeDtypeStruct((depth, width), f32),
            jax.ShapeDtypeStruct(right.shape, f32),
            jax.ShapeDtypeStruct(momentum.shape, f32),
            jax.ShapeDtypeStruct(master.shape, f32),
            jax.ShapeDtypeStruct((depth, width), bf16),
            jax.ShapeDtypeStruct(table.shape, bf16),
        ),
        in_specs=[vmem] * 8,
        out_specs=(hbm,) * 6,
        scratch_shapes=[
            pltpu.VMEM(momentum.shape, f32),
            pltpu.VMEM(master.shape, f32),
            pltpu.VMEM((depth, width), bf16),
            pltpu.SemaphoreType.DMA((shards,)),
            pltpu.SemaphoreType.DMA((5,)),
        ],
        compiler_params=pltpu.CompilerParams(vmem_limit_bytes=30 * 2**20),
        name="apply_update",
    )(corrected, left, right, total, base, momentum, master, table)


def solution(mesh):
    shards, tensors, sections = (mesh.shape[a] for a in ("shard", "tensor", "section"))
    sizes = (shards, tensors, sections)

    def on_device(
        hidden_acts, out_grads, errors, factors, whiten, momentum, master, table, touched_ids, touched_grads
    ):
        power = run_power(
            sizes, table.shape[0], hidden_acts[0], out_grads[0], errors[0, 0], factors[0], whiten[0],
            momentum[0], master[0], table, touched_ids[None], touched_grads,
        )
        depth, width = errors.shape[2:]
        entries = sections * depth * width * tensors
        new_errors, new_factors, new_momentum, new_master, new_weights, new_table = run_update(
            shards, entries, *power
        )
        return (
            new_errors[None, None],
            new_factors[None],
            new_momentum[None],
            new_master[None],
            new_weights[None],
            new_table,
        )

    in_specs = (
        P("section", "shard", "tensor"),
        P("section", "shard", None),
        P("section", "shard", None, "tensor"),
        P("section", None, "tensor"),
        P("section", None, None, None),
        P("section", "shard", "tensor"),
        P("section", "shard", "tensor"),
        P(("shard", "section"), "tensor"),
        P(("shard", "section")),
        P(("shard", "section"), "tensor"),
    )
    out_specs = (
        P("section", "shard", None, "tensor"),
        P("section", None, "tensor"),
        P("section", "shard", "tensor"),
        P("section", "shard", "tensor"),
        P("section", None, "tensor"),
        P(("shard", "section"), "tensor"),
    )
    return jax.shard_map(on_device, mesh=mesh, in_specs=in_specs, out_specs=out_specs, check_vma=False)
```
